256 devices in a mesh: dp: 16 (over z_hi, x, core), expert: 16 (over y, z_lo).
Axes of the slice: x: 4, y: 4, z: 8 (z_hi: 2, z_lo: 4; z = z_hi * 4 + z_lo), core: 2. Of those that a mesh axis runs over, the one named last changes fastest.
Arguments:
- tokens: bfloat16 [32768, 2048], P(('dp', 'expert')), may hold values from -24 to 24
- routes: int32 [32768, 2], P(('dp', 'expert')), may hold values from 0 to 15, all different within a row; in each aligned block of 128 rows (0 to 127, 128 to 255, ...) at most 32 rows name the same one
- gates: float32 [32768, 2], P(('dp', 'expert')), may hold values from 0.2 to 1
- cotangent: bfloat16 [32768, 2048], P(('dp', 'expert')), may hold values from -6 to 6
- w_gate: bfloat16 [16, 2048, 768], P('expert', 'dp'), may hold values from -0.125 to 0.125
- w_up: bfloat16 [16, 2048, 768], P('expert', 'dp'), may hold values from -0.125 to 0.125
- w_down: bfloat16 [16, 768, 2048], P('expert', None, 'dp'), may hold values from -0.21875 to 0.21875
Outputs:
- output: bfloat16 [32768, 2048], P(('dp', 'expert'))
- grad_tokens: bfloat16 [32768, 2048], P(('dp', 'expert'))
- grad_gates: float32 [32768, 2], P(('dp', 'expert'))
- grad_w_gate: bfloat16 [16, 2048, 768], P('expert', 'dp')
- grad_w_up: bfloat16 [16, 2048, 768], P('expert', 'dp')
- grad_w_down: bfloat16 [16, 768, 2048], P('expert', None, 'dp')
The draws below stay inside these ranges and needn't reach their ends.
Inputs may be any that keep to these rules, and one draw needn't show every extreme that they name: `routes`: each row names 2 different experts. In each aligned block of 128 rows no expert is named by more than 32 rows, a bound that some block reaches.
All inputs are finite; a program needn't handle non-finite values.
Results may differ from the reference program's by a relative error of at most 0.018.
Values may be sent and summed in bfloat16 or wider, within the bound.
No kernel may reach another device: no remote copies, remote signals or barrier semaphores. Data moves between devices by JAX's collectives and lax.ppermute only.
A program may use at most 128 MiB of HBM per device.

```python
import math
import jax
import jax.numpy as jnp
import numpy as np
from jax import lax

D = 2048
FF = 768
TOP = 2
TOK_DEV = 128
EXPERTS = 16
CAP = 32
TOKENS = 32768
N_DP = 16
N_EXPERT = 16


def strengthened(entries, rng, source, target, blocks, factor):
    def block_of(dim):
        return (jnp.arange(entries.shape[dim]) // (entries.shape[dim] // blocks)).reshape((-1,) + (1,) * (entries.ndim - 1 - dim))

    one_side = jax.random.permutation(rng, blocks)[block_of(target)]
    other_side = (block_of(target) + blocks // 2) % blocks
    return jnp.where((block_of(source) == one_side) | (block_of(source) == other_side), factor * entries, entries)


def levels(stream_key, shape, shards, least, top_value):
    gain = 1.0
    for position, shards_of in shards:
        heights = jax.random.uniform(jax.random.fold_in(jax.random.fold_in(stream_key, 6), position), (shards_of,), jnp.float32, least / len(shards), top_value / len(shards))
        gain = gain * jnp.repeat(jnp.exp(heights), shape[position] // shards_of).reshape((-1,) + (1,) * (len(shape) - 1 - position))
    return gain


def assign_block(rng, own, number, rows, number_of, top, limit, skew):
    order = jax.random.permutation(rng, number_of)
    heavy_load, usual = shares(number_of, rows * top, limit, skew, True), shares(number_of, rows * top, limit, skew, False)
    places = jnp.arange(number_of)

    def named(tallies, turn):
        used = int((tallies > 0).sum())
        fixed = max(1, used // 4)
        shifted = fixed + (places - fixed + turn * (used - fixed)) % max(1, number_of - fixed)
        return jnp.zeros((number_of,), jnp.int32).at[order[jnp.where(places < fixed, places, shifted)]].set(jnp.asarray(tallies, jnp.int32))

    tallies = jnp.where(number % 4 == 0, named(heavy_load, number // 4), named(usual, number - number // 4 - 1))
    mixed = jax.random.permutation(jax.random.fold_in(own, 3), number_of)
    giver, taker = mixed[0:number_of // 2 * 2:2], mixed[1:number_of // 2 * 2:2]
    room = jnp.minimum(tallies[giver] - 1, limit - tallies[taker]) // 2
    room = jnp.where((giver == order[0]) | (taker == order[0]) | (tallies[taker] == 0), 0, jnp.maximum(room, 0))
    shifted = jax.random.randint(jax.random.fold_in(own, 4), (number_of // 2,), 0, 1 << 20) % (room + 1)
    tallies = tallies.at[giver].add(-shifted).at[taker].add(shifted)
    items = jnp.searchsorted(jnp.cumsum(tallies), jnp.arange(rows * top), side="right").astype(jnp.int32)
    table = items.reshape(top, rows).T
    table = table[jax.random.permutation(jax.random.fold_in(own, 1), rows)]
    turn = jax.random.randint(jax.random.fold_in(own, 2), (rows, 1), 0, top)
    return jnp.take_along_axis(table, (jnp.arange(top)[None, :] + turn) % top, axis=1)


def shares(number_of, total, bound, slope, full):
    portions = [(1 << 20) // math.isqrt(standing ** slope) + 1 for standing in range(1, number_of + 1)]
    largest = bound if full else min(bound, max(-(-total // number_of), total * portions[0] // sum(portions)))
    least = 1 if total - largest >= number_of - 1 else 0
    counts, rest = [largest] + [least] * (number_of - 1), total - largest - least * (number_of - 1)
    while rest > 0:
        movable = [i for i in range(1, number_of) if counts[i] < largest] or [i for i in range(1, number_of) if counts[i] < bound]
        whole, remaining = sum([portions[i] for i in movable]), rest
        for i in movable:
            extra = min(bound - counts[i], max(1, remaining * portions[i] // whole), rest)
            counts[i] = counts[i] + extra
            rest = rest - extra
    return np.array(counts)


def bell_draw(own_key, shape, scale, most, shards=(), held_as=jnp.bfloat16):
    result = scale * jax.random.normal(own_key, shape, jnp.float32)
    if shards:
        result = result * levels(own_key, shape, shards, -0.22, 0.18)
    return jnp.clip(result, -most, most).astype(held_as)


def bell_draw_with(key, dims, spread, bound, split, heavy, kind=jnp.bfloat16):
    drawn = spread * jax.random.normal(key, dims, jnp.float32)
    if split:
        drawn = drawn * levels(key, dims, split, -0.22, 0.18)
    return jnp.clip(strengthened(drawn, jax.random.fold_in(key, 3), *heavy), -bound, bound).astype(kind)


def setup_inputs(seed: int = 0) -> dict:
    key_list = jax.random.split(jax.random.key(seed), 8)
    tokens = bell_draw_with(key_list[0], (TOKENS, D), 1.0, 24.0, ((0, 256),), (0, 1, 256, 6.0))
    routes_keys = jax.random.split(jax.random.fold_in(key_list[1], 1), TOKENS // TOK_DEV)
    routes_turns = jax.random.permutation(jax.random.fold_in(key_list[1], 3), TOKENS // TOK_DEV)
    routes = jax.vmap(lambda own, number: assign_block(jax.random.fold_in(key_list[1], 2), own, number, TOK_DEV, EXPERTS, TOP, CAP, 2))(routes_keys, routes_turns).reshape((TOKENS, TOP))
    gates = jnp.clip(0.2 + 0.8 * jax.random.uniform(key_list[2], (TOKENS, TOP), jnp.float32) ** levels(key_list[2], (TOKENS, TOP), ((0, 256),), -0.2, 0.2), 0.2, 1.0)
    cotangent = bell_draw(key_list[3], (TOKENS, D), 1.0, 6.0, ((0, 256),))
    w_gate = bell_draw(key_list[4], (EXPERTS, D, FF), D ** -0.5, 0.125, ((0, 16), (1, 16)))
    w_up = bell_draw(key_list[5], (EXPERTS, D, FF), D ** -0.5, 0.125, ((0, 16), (1, 16)))
    w_down = bell_draw(key_list[6], (EXPERTS, FF, D), FF ** -0.5, 0.21875, ((0, 16), (2, 16)))
    return dict(tokens=tokens, routes=routes, gates=gates, cotangent=cotangent, w_gate=w_gate, w_up=w_up, w_down=w_down)


def slot_numbers(flat_ids):
    onehot = (flat_ids[:, None] == jnp.arange(EXPERTS, dtype=jnp.int32)[None, :]).astype(jnp.int32)
    before = jnp.cumsum(onehot, axis=0) - onehot
    return jnp.sum(before * onehot, axis=1).astype(jnp.int32)


def expert_pass(x_in, d_out, w_one, u_one, v_one):
    pre = jnp.dot(x_in, w_one, preferred_element_type=jnp.float32)
    up = jnp.dot(x_in, u_one, preferred_element_type=jnp.float32)
    sig = jax.nn.sigmoid(pre)
    act = pre * sig
    hidden = (act * up).astype(jnp.bfloat16)
    outrow = jnp.dot(hidden, v_one, preferred_element_type=jnp.float32).astype(jnp.bfloat16)
    d_hidden = jnp.dot(d_out, v_one.T, preferred_element_type=jnp.float32)
    d_pre = (d_hidden * up * sig * (1.0 + pre * (1.0 - sig))).astype(jnp.bfloat16)
    d_up = (d_hidden * act).astype(jnp.bfloat16)
    d_rows = (jnp.dot(d_pre, w_one.T, preferred_element_type=jnp.float32)
              + jnp.dot(d_up, u_one.T, preferred_element_type=jnp.float32)).astype(jnp.bfloat16)
    grad_one = jnp.dot(x_in.T, d_pre, preferred_element_type=jnp.float32)
    grad_two = jnp.dot(x_in.T, d_up, preferred_element_type=jnp.float32)
    grad_three = jnp.dot(hidden.T, d_out, preferred_element_type=jnp.float32)
    return outrow, d_rows, grad_one, grad_two, grad_three


def reference(tokens, routes, gates, cotangent, w_gate, w_up, w_down):
    per_row = N_EXPERT * TOK_DEV
    width = tokens.shape[1]
    rows = N_EXPERT * CAP
    x_all = tokens.reshape(N_DP, per_row, width)
    id_all = routes.reshape(N_DP, per_row, TOP)
    gate_all = gates.reshape(N_DP, per_row, TOP)
    dy_all = cotangent.reshape(N_DP, per_row, width)

    def row_step(carry, inputs):
        x_row, id_row, gate_row, dy_row = inputs
        blocks = id_row.reshape(N_EXPERT, TOK_DEV * TOP)
        slots = jax.vmap(slot_numbers)(blocks)
        source = jnp.arange(N_EXPERT, dtype=jnp.int32)[:, None]
        place = (blocks * rows + source * CAP + slots).reshape(-1).astype(jnp.int32)
        entry = jnp.arange(per_row * TOP, dtype=jnp.int32)
        table = jnp.zeros((EXPERTS * rows,), jnp.int32).at[place].set(entry)
        live = jnp.zeros((EXPERTS * rows,), jnp.int32).at[place].set(1)
        token_of = (table // TOP).astype(jnp.int32)
        x_buf = jnp.where(live[:, None] > 0, x_row[token_of], jnp.zeros((), jnp.bfloat16))
        d_ent = (gate_row.reshape(-1)[:, None] * jnp.repeat(dy_row.astype(jnp.float32), TOP, axis=0)).astype(jnp.bfloat16)
        d_buf = jnp.where(live[:, None] > 0, d_ent[table], jnp.zeros((), jnp.bfloat16))

        def one_expert(args):
            return expert_pass(*args)

        outrow, d_rows, grad_one, grad_two, grad_three = lax.map(
            one_expert, (x_buf.reshape(EXPERTS, rows, width), d_buf.reshape(EXPERTS, rows, width), w_gate, w_up, w_down))
        parts = []
        for total, grad in zip(carry, (grad_one, grad_two, grad_three)):
            rounded = lax.optimization_barrier(grad.astype(jnp.bfloat16))
            parts.append(total + rounded.astype(jnp.float32))
        o_ent = outrow.reshape(-1, width)[place].astype(jnp.float32).reshape(per_row, TOP, width)
        y_row = jnp.sum(gate_row[:, :, None] * o_ent, axis=1).astype(jnp.bfloat16)
        gg_row = jnp.sum(o_ent * dy_row.astype(jnp.float32)[:, None, :], axis=2)
        dx_row = jnp.sum(d_rows.reshape(-1, width)[place].astype(jnp.float32).reshape(per_row, TOP, width), axis=1).astype(jnp.bfloat16)
        return tuple(parts), (y_row, dx_row, gg_row)

    start = (jnp.zeros(w_gate.shape, jnp.float32), jnp.zeros(w_up.shape, jnp.float32), jnp.zeros(w_down.shape, jnp.float32))
    sums, stacked = lax.scan(row_step, start, (x_all, id_all, gate_all, dy_all))
    y_all, dx_all, gg_all = stacked
    return (y_all.reshape(-1, width), dx_all.reshape(-1, width), gg_all.reshape(-1, TOP),
            sums[0].astype(jnp.bfloat16), sums[1].astype(jnp.bfloat16), sums[2].astype(jnp.bfloat16))
```

```python
import jax
import jax.numpy as jnp
from jax import lax
from jax.experimental import pallas as pl
from jax.experimental.pallas import tpu as pltpu
from jax.sharding import PartitionSpec as P

LANES = 128
F32 = jnp.float32
BF16 = jnp.bfloat16


def slot_numbers(flat_ids, experts):
    onehot = (flat_ids[:, None] == jnp.arange(experts, dtype=jnp.int32)[None, :]).astype(jnp.int32)
    before = jnp.cumsum(onehot, axis=0) - onehot
    return jnp.sum(before * onehot, axis=1)


def neighbour(i, dz, dx, dc):
    z, x, c = i // 8, i // 2 % 4, i % 2
    return ((z ^ dz) * 4 + (x + dx) % 4) * 2 + (c ^ dc)


def push(value, dz=0, dx=0, dc=0):
    pairs = [(i, neighbour(i, dz, dx, dc)) for i in range(16)]
    return lax.ppermute(value, "dp", pairs)


def relative_order():
    table = [
        [neighbour(i, dz, dx, dc) for dc in range(2) for dz in range(2) for dx in range(4)]
        for i in range(16)
    ]
    return jnp.array(table, jnp.int32)[lax.axis_index("dp")]


def gather_pieces(own):
    pieces = {(0, 0, 0): own}
    far = push(own, dz=1)
    pieces[0, 1, 0] = far
    for dz, base in ((0, own), (1, far)):
        pieces[0, dz, 3] = push(base, dx=1)
        pieces[0, dz, 1] = push(base, dx=-1)
        pieces[0, dz, 2] = push(base, dx=2)
    for dz in range(2):
        for dx in range(4):
            pieces[1, dz, dx] = push(pieces[0, dz, dx], dc=1)
    return [pieces[dc, dz, dx] for dc in range(2) for dz in range(2) for dx in range(4)]


def add(*values):
    total = values[0].astype(F32)
    for value in values[1:]:
        total = total + value.astype(F32)
    return total


def scatter_sum(mine, other):
    came = push(other, dc=1)
    both = [
        add(mine[q * LANES : (q + 1) * LANES], came[q * LANES : (q + 1) * LANES]).astype(BF16)
        for q in range(8)
    ]

    def over_x(dz):
        blocks = both[dz * 4 : dz * 4 + 4]
        return add(blocks[0], push(blocks[1], dx=1), push(blocks[3], dx=-1), push(blocks[2], dx=2))

    far = push(over_x(1).astype(BF16), dz=1)
    return add(over_x(0), far).astype(BF16)


def dispatch_kernel(order, pick, row_gate, tokens, cotangent, x_out, d_out, tok, cot):
    for j in range(16):
        source = pl.ds(pl.multiple_of(order[j] * LANES, LANES), LANES)
        tok[:, j * LANES : (j + 1) * LANES] = tokens[:, source]
        cot[:, j * LANES : (j + 1) * LANES] = cotangent[:, source]
    for j in range(4):
        cols = slice(j * 512, (j + 1) * 512)
        x_out[:, cols] = jnp.dot(pick[...], tok[:, cols], preferred_element_type=F32).astype(BF16)
        rows = jnp.dot(pick[...], cot[:, cols], preferred_element_type=F32)
        d_out[:, cols] = (rows * row_gate[...]).astype(BF16)


def dispatch(order, pick, row_gate, tokens, cotangent):
    slots, (rows, width) = pick.shape[0], tokens.shape
    vmem = pl.BlockSpec(memory_space=pltpu.VMEM)
    return pl.pallas_call(
        dispatch_kernel,
        out_shape=[jax.ShapeDtypeStruct((slots, width), BF16)] * 2,
        in_specs=[pl.BlockSpec(memory_space=pltpu.SMEM)] + [vmem] * 4,
        out_specs=[vmem] * 2,
        scratch_shapes=[pltpu.VMEM((rows, width), BF16)] * 2,
        cost_estimate=pl.CostEstimate(
            flops=4 * slots * rows * width, bytes_accessed=5 * slots * width * 2, transcendentals=0
        ),
        name="dispatch",
    )(order, pick, row_gate, tokens, cotangent)


def combine_kernel(order, first, second, gates, back, cotangent, out, grad_gates):
    g0, g1 = gates[:, 0:1], gates[:, 1:2]
    s0 = jnp.zeros((first.shape[0], LANES), F32)
    s1 = jnp.zeros((first.shape[0], LANES), F32)
    for j in range(4):
        cols = slice(j * 512, (j + 1) * 512)
        o0 = jnp.dot(first[...], back[:, cols], preferred_element_type=F32)
        o1 = jnp.dot(second[...], back[:, cols], preferred_element_type=F32)
        y = (g0 * o0 + g1 * o1).astype(BF16)
        for i in range(4):
            part = slice(i * LANES, (i + 1) * LANES)
            target = pl.ds(pl.multiple_of(order[j * 4 + i] * LANES, LANES), LANES)
            out[:, target] = y[:, part]
            dy = cotangent[:, target].astype(F32)
            s0 = s0 + o0[:, part] * dy
            s1 = s1 + o1[:, part] * dy
    grad_gates[:, 0:1] = jnp.sum(s0, axis=1, keepdims=True)
    grad_gates[:, 1:2] = jnp.sum(s1, axis=1, keepdims=True)


def combine(order, first, second, gates, back, cotangent):
    (rows, slots), width = first.shape, back.shape[1]
    vmem = pl.BlockSpec(memory_space=pltpu.VMEM)
    return pl.pallas_call(
        combine_kernel,
        out_shape=[
            jax.ShapeDtypeStruct((rows, width), BF16),
            jax.ShapeDtypeStruct(gates.shape, F32),
        ],
        in_specs=[pl.BlockSpec(memory_space=pltpu.SMEM)] + [vmem] * 5,
        out_specs=[vmem] * 2,
        cost_estimate=pl.CostEstimate(
            flops=4 * slots * rows * width, bytes_accessed=2 * slots * width * 2, transcendentals=0
        ),
        name="combine",
    )(order, first, second, gates, back, cotangent)


def grad_tokens_kernel(order, pick, back, out):
    for j in range(4):
        cols = slice(j * 512, (j + 1) * 512)
        g = jnp.dot(pick[...], back[:, cols], preferred_element_type=F32).astype(BF16)
        for i in range(4):
            target = pl.ds(pl.multiple_of(order[j * 4 + i] * LANES, LANES), LANES)
            out[:, target] = g[:, i * LANES : (i + 1) * LANES]


def combine_grads(order, pick, back):
    (rows, slots), width = pick.shape, back.shape[1]
    vmem = pl.BlockSpec(memory_space=pltpu.VMEM)
    return pl.pallas_call(
        grad_tokens_kernel,
        out_shape=jax.ShapeDtypeStruct((rows, width), BF16),
        in_specs=[pl.BlockSpec(memory_space=pltpu.SMEM)] + [vmem] * 2,
        out_specs=vmem,
        cost_estimate=pl.CostEstimate(
            flops=2 * slots * rows * width, bytes_accessed=2 * slots * width * 2, transcendentals=0
        ),
        name="grad_tokens",
    )(order, pick, back)


def dot_nt(a, b):
    return lax.dot_general(a, b, (((1,), (1,)), ((), ())), preferred_element_type=F32)


def dot_tn(a, b):
    return lax.dot_general(a, b, (((0,), (0,)), ((), ())), preferred_element_type=F32)


def exchange(rows, experts):
    slots, width = rows.shape
    sent = rows.reshape(experts, slots // experts, width)
    return lax.all_to_all(sent, "expert", split_axis=0, concat_axis=0, tiled=True).reshape(slots, width)


def shards(tokens, routes, gates, cotangent, w_gate, w_up, w_down):
    experts = lax.axis_size("expert")
    tok_rows, width = tokens.shape
    top = routes.shape[1]
    hid = w_gate.shape[2]
    half = width // 2
    cap = tok_rows * top * 2 // experts
    order = relative_order()

    own = jnp.concatenate([w_gate[0], w_up[0], w_down[0].T], axis=1)
    pieces = gather_pieces(own)

    flat_ids = routes.reshape(-1)
    target = (flat_ids * cap + slot_numbers(flat_ids, experts)).reshape(tok_rows, top)
    places = jnp.arange(experts * cap, dtype=jnp.int32)
    hit = [places[:, None] == target[None, :, k] for k in range(top)]
    pick = (hit[0] | hit[1]).astype(BF16)
    row_gate = sum(
        jnp.sum(jnp.where(hit[k], gates[None, :, k], 0.0), axis=1, keepdims=True) for k in range(top)
    )
    x_send, d_send = dispatch(order, pick, row_gate, tokens, cotangent)
    x_in = exchange(x_send, experts)
    d_in = exchange(d_send, experts)

    w_gu = jnp.concatenate([piece[:, : 2 * hid] for piece in pieces], axis=0)
    w_dn = jnp.concatenate([piece[:, 2 * hid :] for piece in pieces], axis=0)

    pre_up = jnp.dot(x_in, w_gu, preferred_element_type=F32)
    pre, up = pre_up[:, :hid], pre_up[:, hid:]
    sig = jax.nn.sigmoid(pre)
    act = pre * sig
    hidden = (act * up).astype(BF16)
    out_back = exchange(dot_nt(hidden, w_dn).astype(BF16), experts)

    d_hidden = jnp.dot(d_in, w_dn, preferred_element_type=F32)
    d_pre = (d_hidden * up * sig * (1.0 + pre * (1.0 - sig))).astype(BF16)
    d_up = (d_hidden * act).astype(BF16)
    d_both = jnp.concatenate([d_pre, d_up], axis=1)
    rows_back = exchange(dot_nt(d_both, w_gu).astype(BF16), experts)

    dn_other = dot_tn(d_in[:, half:], hidden).astype(BF16)
    dn_mine = dot_tn(d_in[:, :half], hidden).astype(BF16)
    gu_other = dot_tn(x_in[:, half:], d_both).astype(BF16)
    gu_mine = dot_tn(x_in[:, :half], d_both).astype(BF16)
    g_down = scatter_sum(dn_mine, dn_other)
    g_gu = scatter_sum(gu_mine, gu_other)

    spots = [target[:, k : k + 1] == places[None, :] for k in range(top)]
    first, second = [spot.astype(BF16) for spot in spots]
    output, grad_gates = combine(order, first, second, gates, out_back, cotangent)
    grad_tokens = combine_grads(order, first + second, rows_back)
    return (
        output,
        grad_tokens,
        grad_gates,
        g_gu[None, :, :hid],
        g_gu[None, :, hid:],
        g_down.T[None],
    )


def solution(mesh):
    return jax.shard_map(
        shards,
        mesh=mesh,
        in_specs=(
            P(("dp", "expert"), None),
            P(("dp", "expert"), None),
            P(("dp", "expert"), None),
            P(("dp", "expert"), None),
            P("expert", "dp", None),
            P("expert", "dp", None),
            P("expert", None, "dp"),
        ),
        out_specs=(
            P(("dp", "expert"), None),
            P(("dp", "expert"), None),
            P(("dp", "expert"), None),
            P("expert", "dp", None),
            P("expert", "dp", None),
            P("expert", None, "dp"),
        ),
        check_vma=False,
    )
```

```python
import functools

import jax
import jax.numpy as jnp
import numpy as np
from jax import lax
from jax.experimental import pallas as pl
from jax.experimental.pallas import tpu as pltpu
from jax.sharding import PartitionSpec as P

LANES = 128
F32 = jnp.float32
BF16 = jnp.bfloat16


def slot_numbers(flat_ids, experts):
    onehot = (flat_ids[:, None] == jnp.arange(experts, dtype=jnp.int32)[None, :]).astype(jnp.int32)
    before = jnp.cumsum(onehot, axis=0) - onehot
    return jnp.sum(before * onehot, axis=1)


def neighbour(i, dz, dx, dc):
    z, x, c = i // 8, i // 2 % 4, i % 2
    return ((z ^ dz) * 4 + (x + dx) % 4) * 2 + (c ^ dc)


BLOCKS = [(dc, dz, dx) for dc in range(2) for dz in range(2) for dx in range(4)]


def push(value, dz=0, dx=0, dc=0):
    return lax.ppermute(value, "dp", [(i, neighbour(i, dz, dx, dc)) for i in range(16)])


def z_target(dp, expert, turn):
    shift = (0, 1, -2 if dp % 2 else 2, -1)[turn]
    z = (dp // 8 * 4 + expert % 4 + shift) % 8
    return z // 4 * 8 + dp % 8, expert // 4 * 4 + z % 4


def z_pairs(turn):
    pairs = []
    for i in range(256):
        dp, expert = z_target(i // 16, i % 16, turn)
        pairs.append((i, dp * 16 + expert))
    return pairs


def z_send(value, turn):
    return lax.ppermute(value, ("dp", "expert"), z_pairs(turn))


def z_return(value, turn):
    return lax.ppermute(value, ("dp", "expert"), [(j, i) for i, j in z_pairs(turn)])


def y_send(value, dy):
    return lax.ppermute(value, "expert", [(i, (i + 4 * dy) % 16) for i in range(16)])


def column_spots():
    spots = np.zeros((16, 16), np.int32)
    for i in range(16):
        for j, (dc, dz, dx) in enumerate(BLOCKS):
            spots[i, neighbour(i, dz, dx, dc)] = j
    flips = np.zeros((16, 16, 4), np.int32)
    for i in range(16):
        for e in range(16):
            for turn in range(4):
                flips[i, e, turn] = z_target(i, e, turn)[0] != i
    me, expert = lax.axis_index("dp"), lax.axis_index("expert")
    spots = jnp.array(spots)
    flip = jnp.array(flips.reshape(256, 4))[me * 16 + expert]
    return jnp.where(flip[:, None] != 0, spots[me ^ 8][None, :], spots[me][None, :])


def gather_pieces(own):
    pieces = {(0, 0, 0): own}
    far = push(own, dz=1)
    pieces[0, 1, 0] = far
    for dz, base in ((0, own), (1, far)):
        pieces[0, dz, 3] = push(base, dx=1)
        pieces[0, dz, 1] = push(base, dx=-1)
        pieces[0, dz, 2] = push(base, dx=2)
    for dz in range(2):
        for dx in range(4):
            pieces[1, dz, dx] = push(pieces[0, dz, dx], dc=1)
    return [pieces[block] for block in BLOCKS]


def add(*values):
    total = values[0].astype(F32)
    for value in values[1:]:
        total = total + value.astype(F32)
    return total


def scatter_sum(mine, other):
    came = push(other, dc=1)
    both = [
        add(mine[q * LANES : (q + 1) * LANES], came[q * LANES : (q + 1) * LANES]).astype(BF16)
        for q in range(8)
    ]

    def over_x(dz):
        blocks = both[dz * 4 : dz * 4 + 4]
        return add(blocks[0], push(blocks[1], dx=1), push(blocks[3], dx=-1), push(blocks[2], dx=2))

    far = push(over_x(1).astype(BF16), dz=1)
    return add(over_x(0), far).astype(BF16)


VMEM = pl.BlockSpec(memory_space=pltpu.VMEM)
SMEM = pl.BlockSpec(memory_space=pltpu.SMEM)


def block_cols(j):
    return slice(j * LANES, (j + 1) * LANES)


def spot(spots, turn, j):
    return pl.ds(pl.multiple_of(spots[turn, j] * LANES, LANES), LANES)


def dispatch_kernel(scaled, spots, pick, row_gate, rows, *outs):
    for j in range(4):
        cols = slice(j * 512, (j + 1) * 512)
        moved = jnp.dot(pick[...], rows[:, cols], preferred_element_type=F32)
        if scaled:
            moved = moved * row_gate[...]
        moved = moved.astype(BF16)
        for turn in range(4):
            part = moved[turn * 128 : (turn + 1) * 128]
            for i in range(4):
                outs[turn][:, spot(spots, turn, j * 4 + i)] = part[:, block_cols(i)]


def dispatch(scaled, spots, pick, row_gate, rows):
    slots, (_, width) = pick.shape[0], rows.shape
    return pl.pallas_call(
        functools.partial(dispatch_kernel, scaled),
        out_shape=[jax.ShapeDtypeStruct((slots // 4, width), BF16)] * 4,
        in_specs=[SMEM] + [VMEM] * 3,
        out_specs=[VMEM] * 4,
        cost_estimate=pl.CostEstimate(
            flops=2 * slots * rows.shape[0] * width,
            bytes_accessed=3 * slots * width,
            transcendentals=0,
        ),
        name="dispatch",
    )(spots, pick, row_gate, rows)


def turn_kernel(b0, b1, b2, b3, *outs):
    size = b0.shape[0] // 4
    for i, block in enumerate((b0, b1, b2, b3)):
        for k in range(4):
            outs[k][i * size : (i + 1) * size] = block[k * size : (k + 1) * size]


def turn_blocks(blocks):
    return pl.pallas_call(
        turn_kernel,
        out_shape=[jax.ShapeDtypeStruct(blocks[0].shape, BF16)] * 4,
        in_specs=[VMEM] * 4,
        out_specs=[VMEM] * 4,
        cost_estimate=pl.CostEstimate(
            flops=0, bytes_accessed=16 * blocks[0].size, transcendentals=0
        ),
        name="turn",
    )(*blocks)


def combine_kernel(spots, first, second, gates, b0, b1, b2, b3, cotangent, out, grad_gates, back):
    g0, g1 = gates[:, 0:1], gates[:, 1:2]
    s0 = jnp.zeros((first.shape[0], LANES), F32)
    s1 = jnp.zeros((first.shape[0], LANES), F32)
    for turn, block in enumerate((b0, b1, b2, b3)):
        for j in range(16):
            back[turn * 128 : (turn + 1) * 128, block_cols(j)] = block[:, spot(spots, turn, j)]
    for j in range(4):
        cols = slice(j * 512, (j + 1) * 512)
        o0 = jnp.dot(first[...], back[:, cols], preferred_element_type=F32)
        o1 = jnp.dot(second[...], back[:, cols], preferred_element_type=F32)
        out[:, cols] = (g0 * o0 + g1 * o1).astype(BF16)
        dy = cotangent[:, cols].astype(F32)
        t0, t1 = o0 * dy, o1 * dy
        for i in range(4):
            s0 = s0 + t0[:, block_cols(i)]
            s1 = s1 + t1[:, block_cols(i)]
    grad_gates[:, 0:1] = jnp.sum(s0, axis=1, keepdims=True)
    grad_gates[:, 1:2] = jnp.sum(s1, axis=1, keepdims=True)


def combine(spots, first, second, gates, blocks, cotangent):
    (rows, slots), width = first.shape, cotangent.shape[1]
    return pl.pallas_call(
        combine_kernel,
        out_shape=[
            jax.ShapeDtypeStruct((rows, width), BF16),
            jax.ShapeDtypeStruct(gates.shape, F32),
        ],
        in_specs=[SMEM] + [VMEM] * 8,
        out_specs=[VMEM] * 2,
        scratch_shapes=[pltpu.VMEM((slots, width), BF16)],
        cost_estimate=pl.CostEstimate(
            flops=4 * slots * rows * width, bytes_accessed=2 * slots * width * 2, transcendentals=0
        ),
        name="combine",
    )(spots, first, second, gates, *blocks, cotangent)


def grad_tokens_kernel(spots, pick, b0, b1, b2, b3, out, back):
    for turn, block in enumerate((b0, b1, b2, b3)):
        for j in range(16):
            back[turn * 128 : (turn + 1) * 128, block_cols(j)] = block[:, spot(spots, turn, j)]
    for j in range(4):
        cols = slice(j * 512, (j + 1) * 512)
        out[:, cols] = jnp.dot(pick[...], back[:, cols], preferred_element_type=F32).astype(BF16)


def combine_grads(spots, pick, blocks):
    (rows, slots), width = pick.shape, blocks[0].shape[1]
    return pl.pallas_call(
        grad_tokens_kernel,
        out_shape=jax.ShapeDtypeStruct((rows, width), BF16),
        in_specs=[SMEM] + [VMEM] * 5,
        out_specs=VMEM,
        scratch_shapes=[pltpu.VMEM((slots, width), BF16)],
        cost_estimate=pl.CostEstimate(
            flops=2 * slots * rows * width, bytes_accessed=2 * slots * width * 2, transcendentals=0
        ),
        name="grad_tokens",
    )(spots, pick, *blocks)


def rows_kernel(a, w, *outs):
    size = outs[0].shape[0]
    for j in range(4):
        cols = slice(j * 512, (j + 1) * 512)
        product = lax.dot_general(
            a[...], w[cols, :], (((1,), (1,)), ((), ())), preferred_element_type=F32
        ).astype(BF16)
        for k in range(4):
            outs[k][:, cols] = product[k * size : (k + 1) * size]


def rows_out(a, w):
    (rows, depth), width = a.shape, w.shape[0]
    return pl.pallas_call(
        rows_kernel,
        out_shape=[jax.ShapeDtypeStruct((rows // 4, width), BF16)] * 4,
        in_specs=[VMEM] * 2,
        out_specs=[VMEM] * 4,
        cost_estimate=pl.CostEstimate(
            flops=2 * rows * depth * width,
            bytes_accessed=2 * (rows * depth + width * depth + rows * width),
            transcendentals=0,
        ),
        name="rows_out",
    )(a, w)


def dot_tn(a, b):
    return lax.dot_general(a, b, (((0,), (0,)), ((), ())), preferred_element_type=F32)


def to_experts(blocks):
    met = [blocks[0]] + [z_send(blocks[turn], turn) for turn in range(1, 4)]
    met = turn_blocks(met)
    return jnp.concatenate([met[0]] + [y_send(met[dy], dy) for dy in range(1, 4)], axis=0)


def to_tokens(blocks):
    met = [blocks[0]] + [y_send(blocks[dy], -dy) for dy in range(1, 4)]
    met = turn_blocks(met)
    return [met[0]] + [z_return(met[turn], turn) for turn in range(1, 4)]


def shards(tokens, routes, gates, cotangent, w_gate, w_up, w_down):
    experts = lax.axis_size("expert")
    tok_rows, width = tokens.shape
    top = routes.shape[1]
    hid = w_gate.shape[2]
    half = width // 2
    cap = tok_rows * top * 2 // experts
    spots = column_spots()
    me = lax.axis_index("expert")

    own = jnp.concatenate([w_gate[0], w_up[0], w_down[0].T], axis=1)
    pieces = gather_pieces(own)

    flat_ids = routes.reshape(-1)
    turns, steps = (flat_ids - me) & 3, ((flat_ids >> 2) - (me >> 2)) & 3
    target = (turns * 4 + steps) * cap + slot_numbers(flat_ids, experts)
    target = target.reshape(tok_rows, top)
    places = jnp.arange(experts * cap, dtype=jnp.int32)
    hit = [places[:, None] == target[None, :, k] for k in range(top)]
    pick = (hit[0] | hit[1]).astype(BF16)
    row_gate = sum(
        jnp.sum(jnp.where(hit[k], gates[None, :, k], 0.0), axis=1, keepdims=True) for k in range(top)
    )
    x_in = to_experts(dispatch(False, spots, pick, row_gate, tokens))
    d_in = to_experts(dispatch(True, spots, pick, row_gate, cotangent))

    w_gu = jnp.concatenate([piece[:, : 2 * hid] for piece in pieces], axis=0)
    w_dn = jnp.concatenate([piece[:, 2 * hid :] for piece in pieces], axis=0)

    pre_up = jnp.dot(x_in, w_gu, preferred_element_type=F32)
    pre, up = pre_up[:, :hid], pre_up[:, hid:]
    sig = jax.nn.sigmoid(pre)
    act = pre * sig
    hidden = (act * up).astype(BF16)
    out_back = to_tokens(rows_out(hidden, w_dn))

    d_hidden = jnp.dot(d_in, w_dn, preferred_element_type=F32)
    d_pre = (d_hidden * up * sig * (1.0 + pre * (1.0 - sig))).astype(BF16)
    d_up = (d_hidden * act).astype(BF16)
    d_both = jnp.concatenate([d_pre, d_up], axis=1)
    rows_back = to_tokens(rows_out(d_both, w_gu))

    dn_other = dot_tn(d_in[:, half:], hidden).astype(BF16)
    dn_mine = dot_tn(d_in[:, :half], hidden).astype(BF16)
    gu_other = dot_tn(x_in[:, half:], d_both).astype(BF16)
    gu_mine = dot_tn(x_in[:, :half], d_both).astype(BF16)
    g_down = scatter_sum(dn_mine, dn_other)
    g_gu = scatter_sum(gu_mine, gu_other)

    first, second = [(target[:, k : k + 1] == places[None, :]).astype(BF16) for k in range(top)]
    output, grad_gates = combine(spots, first, second, gates, out_back, cotangent)
    grad_tokens = combine_grads(spots, first + second, rows_back)
    return (
        output,
        grad_tokens,
        grad_gates,
        g_gu[None, :, :hid],
        g_gu[None, :, hid:],
        g_down.T[None],
    )


def solution(mesh):
    return jax.shard_map(
        shards,
        mesh=mesh,
        in_specs=(
            P(("dp", "expert"), None),
            P(("dp", "expert"), None),
            P(("dp", "expert"), None),
            P(("dp", "expert"), None),
            P("expert", "dp", None),
            P("expert", "dp", None),
            P("expert", None, "dp"),
        ),
        out_specs=(
            P(("dp", "expert"), None),
            P(("dp", "expert"), None),
            P(("dp", "expert"), None),
            P("expert", "dp", None),
            P("expert", "dp", None),
            P("expert", None, "dp"),
        ),
        check_vma=False,
    )
```

```python
import functools

import jax
import jax.numpy as jnp
import numpy as np
from jax import lax
from jax.experimental import pallas as pl
from jax.experimental.pallas import tpu as pltpu
from jax.sharding import PartitionSpec as P

LANES = 128
F32 = jnp.float32
BF16 = jnp.bfloat16
VMEM = pl.BlockSpec(memory_space=pltpu.VMEM)
SMEM = pl.BlockSpec(memory_space=pltpu.SMEM)


def neighbour(i, dz, dx, dc):
    z, x, c = i // 8, i // 2 % 4, i % 2
    return ((z ^ dz) * 4 + (x + dx) % 4) * 2 + (c ^ dc)


BLOCKS = [(dc, dz, dx) for dc in range(2) for dz in range(2) for dx in range(4)]


def push(value, dz=0, dx=0, dc=0):
    return lax.ppermute(value, "dp", [(i, neighbour(i, dz, dx, dc)) for i in range(16)])


def z_target(dp, expert, turn):
    shift = (0, 1, -2 if dp % 2 else 2, -1)[turn]
    z = (dp // 8 * 4 + expert % 4 + shift) % 8
    return z // 4 * 8 + dp % 8, expert // 4 * 4 + z % 4


def z_pairs(turn):
    pairs = []
    for i in range(256):
        dp, expert = z_target(i // 16, i % 16, turn)
        pairs.append((i, dp * 16 + expert))
    return pairs


def z_send(value, turn):
    return lax.ppermute(value, ("dp", "expert"), z_pairs(turn))


def z_return(value, turn):
    return lax.ppermute(value, ("dp", "expert"), [(j, i) for i, j in z_pairs(turn)])


def y_send(value, dy):
    return lax.ppermute(value, "expert", [(i, (i + 4 * dy) % 16) for i in range(16)])


def column_spots():
    spots = np.zeros((16, 16), np.int32)
    for i in range(16):
        for j, (dc, dz, dx) in enumerate(BLOCKS):
            spots[i, neighbour(i, dz, dx, dc)] = j
    table = np.zeros((256, 4, 16), np.int32)
    for i in range(256):
        for turn in range(4):
            table[i, turn] = spots[z_target(i // 16, i % 16, turn)[0]]
    return jnp.array(table)[lax.axis_index("dp") * 16 + lax.axis_index("expert")]


def add(*values):
    total = values[0].astype(F32)
    for value in values[1:]:
        total = total + value.astype(F32)
    return total


def block_cols(j):
    return slice(j * LANES, (j + 1) * LANES)


def spot(spots, turn, j):
    return pl.ds(pl.multiple_of(spots[turn, j] * LANES, LANES), LANES)


def place_in_buffer(me, cap, experts, routes):
    tokens = routes.shape[1]
    lanes = [routes[k : k + 1, :] for k in range(2)]
    kinds = lax.broadcasted_iota(jnp.int32, (experts, tokens), 0)
    hits = [(kinds == lane).astype(F32) for lane in lanes]
    earlier = lax.broadcasted_iota(jnp.int32, (tokens, tokens), 0) < lax.broadcasted_iota(
        jnp.int32, (tokens, tokens), 1
    )
    counts = jnp.dot(
        (hits[0] + hits[1]).astype(BF16),
        earlier.astype(F32).astype(BF16),
        preferred_element_type=F32,
    )
    targets = []
    for k in range(2):
        slot = jnp.sum(counts * hits[k], axis=0, keepdims=True).astype(jnp.int32)
        turns, steps = (lanes[k] - me) & 3, ((lanes[k] >> 2) - (me >> 2)) & 3
        targets.append((turns * 4 + steps) * cap + slot)
    return targets


def send_kernel(by_turn, cap, experts, spots, me, routes, gates, rows, *outs):
    targets = place_in_buffer(me[0], cap, experts, routes[...])
    spots_of = lax.broadcasted_iota(jnp.int32, (experts * cap, rows.shape[0]), 0)
    hits = [spots_of == target for target in targets]
    pick = jnp.where(hits[0] | hits[1], 1.0, 0.0).astype(BF16)
    if by_turn:
        outs[4][0:1, :], outs[4][1:2, :] = targets
    else:
        weight = jnp.where(hits[0], gates[0:1, :], 0.0) + jnp.where(hits[1], gates[1:2, :], 0.0)
        row_gate = jnp.sum(weight, axis=1, keepdims=True)
    for j in range(4):
        moved = jnp.dot(pick, rows[:, j * 512 : (j + 1) * 512], preferred_element_type=F32)
        if not by_turn:
            moved = moved * row_gate
        moved = moved.astype(BF16)
        for i in range(4):
            for turn in range(4):
                cols = spot(spots, turn, j * 4 + i)
                part = moved[turn * 4 * cap : (turn + 1) * 4 * cap, block_cols(i)]
                if by_turn:
                    outs[turn][:, cols] = part
                else:
                    for step in range(4):
                        outs[step][turn * cap : (turn + 1) * cap, cols] = part[
                            step * cap : (step + 1) * cap
                        ]


def send(by_turn, spots, routes, gates, rows):
    (tokens, width), experts = rows.shape, lax.axis_size("expert")
    cap = tokens * routes.shape[0] * 2 // experts
    slots = experts * cap
    shapes = [jax.ShapeDtypeStruct((slots // 4, width), BF16)] * 4
    if by_turn:
        shapes = shapes + [jax.ShapeDtypeStruct(routes.shape, jnp.int32)]
    return pl.pallas_call(
        functools.partial(send_kernel, by_turn, cap, experts),
        out_shape=shapes,
        in_specs=[SMEM] * 2 + [VMEM] * 3,
        out_specs=[VMEM] * len(shapes),
        cost_estimate=pl.CostEstimate(
            flops=2 * slots * tokens * width, bytes_accessed=3 * slots * width, transcendentals=0
        ),
        name="send",
    )(spots, lax.axis_index("expert").reshape(1), routes, gates, rows)


def turn_kernel(b0, b1, b2, b3, *outs):
    size = b0.shape[0] // 4
    for i, block in enumerate((b0, b1, b2, b3)):
        for k in range(4):
            outs[k][i * size : (i + 1) * size] = block[k * size : (k + 1) * size]


def turn_blocks(blocks):
    return pl.pallas_call(
        turn_kernel,
        out_shape=[jax.ShapeDtypeStruct(blocks[0].shape, BF16)] * 4,
        in_specs=[VMEM] * 4,
        out_specs=[VMEM] * 4,
        cost_estimate=pl.CostEstimate(
            flops=0, bytes_accessed=16 * blocks[0].size, transcendentals=0
        ),
        name="turn",
    )(*blocks)


NT = (((1,), (1,)), ((), ()))
TN = (((0,), (0,)), ((), ()))


def chunk(n, size):
    return pl.ds(pl.multiple_of(n * size, size), size)


def forward_kernel(b0, b1, b2, b3, near, other, x_in, hidden, act, slope, *outs):
    size, hid = b0.shape[0], hidden.shape[1]
    half = near.shape[0]
    for k, block in enumerate((b0, b1, b2, b3)):
        x_in[k * size : (k + 1) * size] = block[...]

    @pl.loop(0, hid // 256)
    def _(n):
        cols, up_cols = chunk(n, 256), pl.ds(pl.multiple_of(hid + n * 256, 256), 256)

        def product(where):
            return jnp.dot(
                x_in[:, :half], near[:, where], preferred_element_type=F32
            ) + jnp.dot(x_in[:, half:], other[:, where], preferred_element_type=F32)

        pre, up = product(cols), product(up_cols)
        sig = jax.nn.sigmoid(pre)
        silu = pre * sig
        act[:, cols] = silu
        slope[:, cols] = up * sig * (1.0 + pre * (1.0 - sig))
        hidden[:, cols] = (silu * up).astype(BF16)

    @pl.loop(0, half // 512)
    def _(n):
        for w, first in ((near, 0), (other, half)):
            rows = lax.dot_general(
                hidden[...], w[chunk(n, 512), 2 * hid :], NT, preferred_element_type=F32
            ).astype(BF16)
            cols = pl.ds(pl.multiple_of(first + n * 512, 512), 512)
            for k in range(4):
                outs[k][:, cols] = rows[k * size : (k + 1) * size]


def forward(blocks, near, other, hid):
    (rows, width) = blocks[0].shape
    whole = 4 * rows
    return pl.pallas_call(
        forward_kernel,
        out_shape=[
            jax.ShapeDtypeStruct((whole, width), BF16),
            jax.ShapeDtypeStruct((whole, hid), BF16),
            jax.ShapeDtypeStruct((whole, hid), F32),
            jax.ShapeDtypeStruct((whole, hid), F32),
        ]
        + [jax.ShapeDtypeStruct((rows, width), BF16)] * 4,
        in_specs=[VMEM] * 6,
        out_specs=[VMEM] * 8,
        cost_estimate=pl.CostEstimate(
            flops=6 * whole * width * hid,
            bytes_accessed=6 * width * hid + 6 * whole * width + 10 * whole * hid,
            transcendentals=whole * hid,
        ),
        name="forward",
    )(*blocks, near, other)


def backward_kernel(b0, b1, b2, b3, near, other, act, slope, d_in, d_both, *outs):
    cap, hid = b0.shape[0] // 4, act.shape[1]
    half = near.shape[0]
    for turn, block in enumerate((b0, b1, b2, b3)):
        for step in range(4):
            row = (step * 4 + turn) * cap
            d_in[row : row + cap] = block[step * cap : (step + 1) * cap]

    @pl.loop(0, hid // 256)
    def _(n):
        cols, up_cols = chunk(n, 256), pl.ds(pl.multiple_of(hid + n * 256, 256), 256)
        where = pl.ds(pl.multiple_of(2 * hid + n * 256, 256), 256)
        d_hidden = jnp.dot(
            d_in[:, :half], near[:, where], preferred_element_type=F32
        ) + jnp.dot(d_in[:, half:], other[:, where], preferred_element_type=F32)
        d_both[:, cols] = (d_hidden * slope[:, cols]).astype(BF16)
        d_both[:, up_cols] = (d_hidden * act[:, cols]).astype(BF16)

    @pl.loop(0, half // 512)
    def _(n):
        for w, first in ((near, 0), (other, half)):
            rows = lax.dot_general(
                d_both[...], w[chunk(n, 512), : 2 * hid], NT, preferred_element_type=F32
            ).astype(BF16)
            cols = pl.ds(pl.multiple_of(first + n * 512, 512), 512)
            for turn in range(4):
                for step in range(4):
                    row = (step * 4 + turn) * cap
                    outs[turn][step * cap : (step + 1) * cap, cols] = rows[row : row + cap]


def backward(blocks, near, other, act, slope):
    (rows, width), (whole, hid) = blocks[0].shape, act.shape
    return pl.pallas_call(
        backward_kernel,
        out_shape=[
            jax.ShapeDtypeStruct((whole, width), BF16),
            jax.ShapeDtypeStruct((whole, 2 * hid), BF16),
        ]
        + [jax.ShapeDtypeStruct((rows, width), BF16)] * 4,
        in_specs=[VMEM] * 8,
        out_specs=[VMEM] * 6,
        cost_estimate=pl.CostEstimate(
            flops=6 * whole * width * hid,
            bytes_accessed=6 * width * hid + 6 * whole * width + 12 * whole * hid,
            transcendentals=0,
        ),
        name="backward",
    )(*blocks, near, other, act, slope)


def fold_kernel(gu_mine, dn_mine, gu_came, dn_came, *outs):
    hid2 = gu_mine.shape[1]
    for q in range(4):
        rows = slice(q * LANES, (q + 1) * LANES)
        outs[q][:, :hid2] = add(gu_mine[rows], gu_came[rows]).astype(BF16)
        outs[q][:, hid2:] = add(dn_mine[rows], dn_came[rows]).astype(BF16)


def fold(dz, *parts):
    columns = [part.shape[1] for part in parts]
    total = columns[0] + columns[1]
    return pl.pallas_call(
        fold_kernel,
        grid=(1,),
        out_shape=[jax.ShapeDtypeStruct((LANES, total), BF16)] * 4,
        in_specs=[pl.BlockSpec((4 * LANES, n), lambda i: (dz, 0)) for n in columns],
        out_specs=[pl.BlockSpec((LANES, total), lambda i: (0, 0))] * 4,
        cost_estimate=pl.CostEstimate(
            flops=4 * LANES * total, bytes_accessed=24 * LANES * total, transcendentals=0
        ),
        name="fold",
    )(*parts)


def picks(targets, slots):
    rows = lax.broadcasted_iota(jnp.int32, (slots, targets.shape[1]), 0)
    return [rows == targets[k : k + 1, :] for k in range(2)]


def combine_kernel(spots, targets, gates, b0, b1, b2, b3, cotangent, out, grad_gates, back):
    for turn, block in enumerate((b0, b1, b2, b3)):
        for j in range(16):
            back[turn * 128 : (turn + 1) * 128, block_cols(j)] = block[:, spot(spots, turn, j)]
    tokens = out.shape[0]
    first, second = [
        jnp.where(hit, 1.0, 0.0).astype(BF16) for hit in picks(targets[...], back.shape[0])
    ]
    g0, g1 = gates[:, 0:1], gates[:, 1:2]
    s0 = jnp.zeros((tokens, LANES), F32)
    s1 = jnp.zeros((tokens, LANES), F32)
    for j in range(4):
        cols = slice(j * 512, (j + 1) * 512)
        o0 = lax.dot_general(first, back[:, cols], TN, preferred_element_type=F32)
        o1 = lax.dot_general(second, back[:, cols], TN, preferred_element_type=F32)
        out[:, cols] = (g0 * o0 + g1 * o1).astype(BF16)
        dy = cotangent[:, cols].astype(F32)
        t0, t1 = o0 * dy, o1 * dy
        for i in range(4):
            s0 = s0 + t0[:, block_cols(i)]
            s1 = s1 + t1[:, block_cols(i)]
    grad_gates[:, 0:1] = jnp.sum(s0, axis=1, keepdims=True)
    grad_gates[:, 1:2] = jnp.sum(s1, axis=1, keepdims=True)


def combine(spots, targets, gates, blocks, cotangent):
    (rows, width), slots = cotangent.shape, 4 * blocks[0].shape[0]
    return pl.pallas_call(
        combine_kernel,
        out_shape=[
            jax.ShapeDtypeStruct((rows, width), BF16),
            jax.ShapeDtypeStruct(gates.shape, F32),
        ],
        in_specs=[SMEM] + [VMEM] * 7,
        out_specs=[VMEM] * 2,
        scratch_shapes=[pltpu.VMEM((slots, width), BF16)],
        cost_estimate=pl.CostEstimate(
            flops=4 * slots * rows * width, bytes_accessed=2 * slots * width * 2, transcendentals=0
        ),
        name="combine",
    )(spots, targets, gates, *blocks, cotangent)


def grad_tokens_kernel(spots, targets, b0, b1, b2, b3, out, back):
    cap = b0.shape[0] // 4
    for step, block in enumerate((b0, b1, b2, b3)):
        for turn in range(4):
            row = (turn * 4 + step) * cap
            for j in range(16):
                back[row : row + cap, block_cols(j)] = block[
                    turn * cap : (turn + 1) * cap, spot(spots, turn, j)
                ]
    hits = picks(targets[...], back.shape[0])
    pick = jnp.where(hits[0] | hits[1], 1.0, 0.0).astype(BF16)
    for j in range(4):
        cols = slice(j * 512, (j + 1) * 512)
        out[:, cols] = lax.dot_general(
            pick, back[:, cols], TN, preferred_element_type=F32
        ).astype(BF16)


def combine_grads(spots, targets, blocks):
    width, slots, rows = blocks[0].shape[1], 4 * blocks[0].shape[0], targets.shape[1]
    return pl.pallas_call(
        grad_tokens_kernel,
        out_shape=jax.ShapeDtypeStruct((rows, width), BF16),
        in_specs=[SMEM] + [VMEM] * 5,
        out_specs=VMEM,
        scratch_shapes=[pltpu.VMEM((slots, width), BF16)],
        cost_estimate=pl.CostEstimate(
            flops=2 * slots * rows * width, bytes_accessed=2 * slots * width * 2, transcendentals=0
        ),
        name="grad_tokens",
    )(spots, targets, *blocks)


def dot_tn(a, b):
    return lax.dot_general(a, b, TN, preferred_element_type=F32)


def over_z(mover, blocks):
    return [blocks[0]] + [mover(blocks[turn], turn) for turn in range(1, 4)]


def over_y(sign, blocks):
    return [blocks[0]] + [y_send(blocks[dy], sign * dy) for dy in range(1, 4)]


def over_x(value):
    return {3: push(value, dx=1), 1: push(value, dx=-1), 2: push(value, dx=2)}


def shards(tokens, routes, gates, cotangent, w_gate, w_up, w_down):
    hid = w_gate.shape[2]
    half = tokens.shape[1] // 2
    spots = column_spots()
    routes_t, gates_t = routes.T, gates.T

    own = jnp.concatenate([w_gate[0], w_up[0], w_down[0].T], axis=1)
    far = push(own, dz=1)

    *x_sent, targets = send(True, spots, routes_t, gates_t, tokens)
    x_met = over_z(z_send, x_sent)
    d_sent = send(False, spots, routes_t, gates_t, cotangent)
    d_met = over_y(1, d_sent)

    near_x = over_x(own)
    far_x = over_x(far)
    near = jnp.concatenate(
        [own] + [near_x[i] for i in (1, 2, 3)] + [far] + [far_x[i] for i in (1, 2, 3)], axis=0
    )
    other = push(near, dc=1)

    d_met = turn_blocks(d_met)
    d_blocks = over_z(z_send, d_met)
    x_met = turn_blocks(x_met)
    x_blocks = over_y(1, x_met)

    x_in, hidden, act, slope, *o_sent = forward(x_blocks, near, other, hid)
    o_met = over_y(-1, o_sent)
    d_in, d_both, *r_sent = backward(d_blocks, near, other, act, slope)
    r_met = over_z(z_return, r_sent)

    gu_other = dot_tn(x_in[:, half:], d_both).astype(BF16)
    dn_other = dot_tn(d_in[:, half:], hidden).astype(BF16)
    gu_came, dn_came = push(gu_other, dc=1), push(dn_other, dc=1)
    gu_mine = dot_tn(x_in[:, :half], d_both).astype(BF16)
    dn_mine = dot_tn(d_in[:, :half], hidden).astype(BF16)

    def sum_over_x(dz):
        mine, *rest = fold(dz, gu_mine, dn_mine, gu_came, dn_came)
        came = push(rest[0], dx=1), push(rest[2], dx=-1), push(rest[1], dx=2)
        return add(mine, *came)

    far_sum = sum_over_x(1).astype(BF16)
    far_sum = push(far_sum, dz=1)
    grads = add(sum_over_x(0), far_sum).astype(BF16)

    o_met = turn_blocks(o_met)
    o_blocks = over_z(z_return, o_met)
    r_met = turn_blocks(r_met)
    r_blocks = over_y(-1, r_met)
    output, grad_gates = combine(spots, targets, gates, o_blocks, cotangent)
    grad_tokens = combine_grads(spots, targets, r_blocks)
    return (
        output,
        grad_tokens,
        grad_gates,
        grads[None, :, :hid],
        grads[None, :, hid : 2 * hid],
        grads[:, 2 * hid :].T[None],
    )


def solution(mesh):
    return jax.shard_map(
        shards,
        mesh=mesh,
        in_specs=(
            P(("dp", "expert"), None),
            P(("dp", "expert"), None),
            P(("dp", "expert"), None),
            P(("dp", "expert"), None),
            P("expert", "dp", None),
            P("expert", "dp", None),
            P("expert", None, "dp"),
        ),
        out_specs=(
            P(("dp", "expert"), None),
            P(("dp", "expert"), None),
            P(("dp", "expert"), None),
            P("expert", "dp", None),
            P("expert", "dp", None),
            P("expert", None, "dp"),
        ),
        check_vma=False,
    )
```

```python
import functools

import jax
import jax.numpy as jnp
import numpy as np
from jax import lax
from jax.experimental import pallas as pl
from jax.experimental.pallas import tpu as pltpu
from jax.sharding import PartitionSpec as P

LANES = 128
F32 = jnp.float32
BF16 = jnp.bfloat16
VMEM = pl.BlockSpec(memory_space=pltpu.VMEM)
SMEM = pl.BlockSpec(memory_space=pltpu.SMEM)


BLOCKS = [(dc, dz, x) for dc in range(2) for dz in range(2) for x in range(4)]


def push(value, dz=0, dc=0):
    return lax.ppermute(value, "dp", [(i, i ^ (8 * dz + dc)) for i in range(16)])


X_GROUPS = [[(zh * 4 + x) * 2 + c for x in range(4)] for zh in range(2) for c in range(2)]


def over_x(blocks):
    return lax.all_to_all(
        blocks, "dp", split_axis=0, concat_axis=0, tiled=True, axis_index_groups=X_GROUPS
    )


def z_target(dp, expert, turn):
    shift = (0, 1, -2 if dp % 2 else 2, -1)[turn]
    z = (dp // 8 * 4 + expert % 4 + shift) % 8
    return z // 4 * 8 + dp % 8, expert // 4 * 4 + z % 4


def z_pairs(turn):
    pairs = []
    for i in range(256):
        dp, expert = z_target(i // 16, i % 16, turn)
        pairs.append((i, dp * 16 + expert))
    return pairs


def z_send(value, turn):
    return lax.ppermute(value, ("dp", "expert"), z_pairs(turn))


def z_return(value, turn):
    return lax.ppermute(value, ("dp", "expert"), [(j, i) for i, j in z_pairs(turn)])


def y_send(value, dy):
    return lax.ppermute(value, "expert", [(i, (i + 4 * dy) % 16) for i in range(16)])


def column_spots():
    spots = np.zeros((16, 16), np.int32)
    for i in range(16):
        for j, (dc, dz, x) in enumerate(BLOCKS):
            spots[i, ((i // 8 ^ dz) * 4 + x) * 2 + (i % 2 ^ dc)] = j
    table = np.zeros((256, 4, 16), np.int32)
    for i in range(256):
        for turn in range(4):
            table[i, turn] = spots[z_target(i // 16, i % 16, turn)[0]]
    return jnp.array(table)[lax.axis_index("dp") * 16 + lax.axis_index("expert")]


def add(*values):
    total = values[0].astype(F32)
    for value in values[1:]:
        total = total + value.astype(F32)
    return total


def block_cols(j):
    return slice(j * LANES, (j + 1) * LANES)


def spot(spots, turn, j):
    return pl.ds(pl.multiple_of(spots[turn, j] * LANES, LANES), LANES)


def place_in_buffer(me, cap, experts, routes):
    tokens = routes.shape[1]
    lanes = [routes[k : k + 1, :] for k in range(2)]
    kinds = lax.broadcasted_iota(jnp.int32, (experts, tokens), 0)
    hits = [(kinds == lane).astype(F32) for lane in lanes]
    earlier = lax.broadcasted_iota(jnp.int32, (tokens, tokens), 0) < lax.broadcasted_iota(
        jnp.int32, (tokens, tokens), 1
    )
    counts = jnp.dot(
        (hits[0] + hits[1]).astype(BF16),
        earlier.astype(F32).astype(BF16),
        preferred_element_type=F32,
    )
    targets = []
    for k in range(2):
        slot = jnp.sum(counts * hits[k], axis=0, keepdims=True).astype(jnp.int32)
        turns, steps = (lanes[k] - me) & 3, ((lanes[k] >> 2) - (me >> 2)) & 3
        targets.append((turns * 4 + steps) * cap + slot)
    return targets


def send_kernel(by_turn, cap, experts, spots, me, routes, gates, rows, *outs):
    targets = place_in_buffer(me[0], cap, experts, routes[...])
    spots_of = lax.broadcasted_iota(jnp.int32, (experts * cap, rows.shape[0]), 0)
    hits = [spots_of == target for target in targets]
    pick = jnp.where(hits[0] | hits[1], 1.0, 0.0).astype(BF16)
    if by_turn:
        outs[4][0:1, :], outs[4][1:2, :] = targets
    else:
        weight = jnp.where(hits[0], gates[0:1, :], 0.0) + jnp.where(hits[1], gates[1:2, :], 0.0)
        row_gate = jnp.sum(weight, axis=1, keepdims=True)
    for j in range(4):
        moved = jnp.dot(pick, rows[:, j * 512 : (j + 1) * 512], preferred_element_type=F32)
        if not by_turn:
            moved = moved * row_gate
        moved = moved.astype(BF16)
        for i in range(4):
            for turn in range(4):
                cols = spot(spots, turn, j * 4 + i)
                part = moved[turn * 4 * cap : (turn + 1) * 4 * cap, block_cols(i)]
                if by_turn:
                    outs[turn][:, cols] = part
                else:
                    for step in range(4):
                        outs[step][turn * cap : (turn + 1) * cap, cols] = part[
                            step * cap : (step + 1) * cap
                        ]


def send(by_turn, spots, routes, gates, rows):
    (tokens, width), experts = rows.shape, lax.axis_size("expert")
    cap = tokens * routes.shape[0] * 2 // experts
    slots = experts * cap
    shapes = [jax.ShapeDtypeStruct((slots // 4, width), BF16)] * 4
    if by_turn:
        shapes = shapes + [jax.ShapeDtypeStruct(routes.shape, jnp.int32)]
    return pl.pallas_call(
        functools.partial(send_kernel, by_turn, cap, experts),
        out_shape=shapes,
        in_specs=[SMEM] * 2 + [VMEM] * 3,
        out_specs=[VMEM] * len(shapes),
        cost_estimate=pl.CostEstimate(
            flops=2 * slots * tokens * width, bytes_accessed=3 * slots * width, transcendentals=0
        ),
        name="send",
    )(spots, lax.axis_index("expert").reshape(1), routes, gates, rows)


def turn_kernel(b0, b1, b2, b3, *outs):
    size = b0.shape[0] // 4
    for i, block in enumerate((b0, b1, b2, b3)):
        for k in range(4):
            outs[k][i * size : (i + 1) * size] = block[k * size : (k + 1) * size]


def turn_blocks(blocks):
    return pl.pallas_call(
        turn_kernel,
        out_shape=[jax.ShapeDtypeStruct(blocks[0].shape, BF16)] * 4,
        in_specs=[VMEM] * 4,
        out_specs=[VMEM] * 4,
        cost_estimate=pl.CostEstimate(
            flops=0, bytes_accessed=16 * blocks[0].size, transcendentals=0
        ),
        name="turn",
    )(*blocks)


NT = (((1,), (1,)), ((), ()))
TN = (((0,), (0,)), ((), ()))


def chunk(n, size):
    return pl.ds(pl.multiple_of(n * size, size), size)


def quarter_dot(a, quarters, where):
    depth = quarters[0].shape[0]
    total = None
    for q, w in enumerate(quarters):
        part = jnp.dot(
            a[:, q * depth : (q + 1) * depth], w[:, where], preferred_element_type=F32
        )
        total = part if total is None else total + part
    return total


def forward_kernel(b0, b1, b2, b3, w0, w1, w2, w3, x_in, hidden, act, slope, *outs):
    size, hid = b0.shape[0], hidden.shape[1]
    quarters = (w0, w1, w2, w3)
    for k, block in enumerate((b0, b1, b2, b3)):
        x_in[k * size : (k + 1) * size] = block[...]

    @pl.loop(0, hid // 256)
    def _(n):
        cols, up_cols = chunk(n, 256), pl.ds(pl.multiple_of(hid + n * 256, 256), 256)
        pre, up = quarter_dot(x_in, quarters, cols), quarter_dot(x_in, quarters, up_cols)
        sig = jax.nn.sigmoid(pre)
        silu = pre * sig
        act[:, cols] = silu.astype(BF16)
        slope[:, cols] = (up * sig * (1.0 + pre * (1.0 - sig))).astype(BF16)
        hidden[:, cols] = (silu * up).astype(BF16)

    for q, w in enumerate(quarters):
        rows = lax.dot_general(
            hidden[...], w[:, 2 * hid :], NT, preferred_element_type=F32
        ).astype(BF16)
        for k in range(4):
            outs[k][:, q * 512 : (q + 1) * 512] = rows[k * size : (k + 1) * size]


def forward(blocks, quarters, hid):
    rows, width = blocks[0].shape
    whole = 4 * rows
    return pl.pallas_call(
        forward_kernel,
        out_shape=[jax.ShapeDtypeStruct((whole, width), BF16)]
        + [jax.ShapeDtypeStruct((whole, hid), BF16)] * 3
        + [jax.ShapeDtypeStruct((rows, width), BF16)] * 4,
        in_specs=[VMEM] * 8,
        out_specs=[VMEM] * 8,
        cost_estimate=pl.CostEstimate(
            flops=6 * whole * width * hid,
            bytes_accessed=6 * width * hid + 6 * whole * width + 6 * whole * hid,
            transcendentals=whole * hid,
        ),
        name="forward",
    )(*blocks, *quarters)


def hidden_kernel(b0, b1, b2, b3, w0, w1, w2, w3, act, slope, d_in, d_both):
    cap, hid = b0.shape[0] // 4, act.shape[1]
    for turn, block in enumerate((b0, b1, b2, b3)):
        for step in range(4):
            row = (step * 4 + turn) * cap
            d_in[row : row + cap] = block[step * cap : (step + 1) * cap]

    @pl.loop(0, hid // 256)
    def _(n):
        cols, up_cols = chunk(n, 256), pl.ds(pl.multiple_of(hid + n * 256, 256), 256)
        d_hidden = quarter_dot(d_in, (w0, w1, w2, w3), cols)
        d_both[:, cols] = (d_hidden * slope[:, cols].astype(F32)).astype(BF16)
        d_both[:, up_cols] = (d_hidden * act[:, cols].astype(F32)).astype(BF16)


def whole_spec(shape):
    return pl.BlockSpec(shape, lambda *_: (0,) * len(shape))


def hidden_grads(blocks, quarters, act, slope):
    (rows, width), (whole, hid) = blocks[0].shape, act.shape
    return pl.pallas_call(
        hidden_kernel,
        grid=(1,),
        out_shape=[
            jax.ShapeDtypeStruct((whole, width), BF16),
            jax.ShapeDtypeStruct((whole, 2 * hid), BF16),
        ],
        in_specs=[whole_spec((rows, width))] * 4
        + [pl.BlockSpec((width // 4, hid), lambda i: (0, 2))] * 4
        + [whole_spec((whole, hid))] * 2,
        out_specs=[whole_spec((whole, width)), whole_spec((whole, 2 * hid))],
        cost_estimate=pl.CostEstimate(
            flops=2 * whole * width * hid,
            bytes_accessed=2 * width * hid + 4 * whole * width + 8 * whole * hid,
            transcendentals=0,
        ),
        name="hidden_grads",
    )(*blocks, *quarters, act, slope)


def row_grads_kernel(d_both, w0, w1, w2, w3, *outs):
    cap = outs[0].shape[0] // 4
    for q, w in enumerate((w0, w1, w2, w3)):
        rows = lax.dot_general(d_both[...], w[...], NT, preferred_element_type=F32).astype(BF16)
        for turn in range(4):
            for step in range(4):
                row = (step * 4 + turn) * cap
                outs[turn][step * cap : (step + 1) * cap, q * 512 : (q + 1) * 512] = rows[
                    row : row + cap
                ]


def row_grads(d_both, quarters):
    (whole, both), width = d_both.shape, 4 * quarters[0].shape[0]
    return pl.pallas_call(
        row_grads_kernel,
        grid=(1,),
        out_shape=[jax.ShapeDtypeStruct((whole // 4, width), BF16)] * 4,
        in_specs=[whole_spec((whole, both))]
        + [pl.BlockSpec((width // 4, both), lambda i: (0, 0))] * 4,
        out_specs=[whole_spec((whole // 4, width))] * 4,
        cost_estimate=pl.CostEstimate(
            flops=2 * whole * width * both,
            bytes_accessed=2 * (width * both + whole * width + whole * both),
            transcendentals=0,
        ),
        name="row_grads",
    )(d_both, *quarters)


def weight_grads_kernel(adds, base, x_in, d_in, d_both, hidden, *refs):
    out = refs[-1]

    def put(value):
        out[...] = (value + refs[0][...].astype(F32) if adds else value).astype(BF16)

    @pl.when(pl.program_id(0) < 2)
    def _():
        put(lax.dot_general(x_in[...], d_both[...], TN, preferred_element_type=F32))

    @pl.when(pl.program_id(0) == 2)
    def _():
        put(lax.dot_general(d_in[...], hidden[...], TN, preferred_element_type=F32))


def weight_grads(quarter, x_in, d_in, d_both, hidden, came=None):
    (whole, width), hid = x_in.shape, hidden.shape[1]
    size = width // 4
    columns = pl.BlockSpec((whole, size), lambda n, base: (0, base[0]))
    third = pl.BlockSpec((size, hid), lambda n, base: (0, n))
    inputs = [x_in, d_in, d_both, hidden] + ([] if came is None else [came])
    specs = [
        columns,
        columns,
        pl.BlockSpec((whole, hid), lambda n, base: (0, jnp.minimum(n, 1))),
        pl.BlockSpec((whole, hid), lambda n, base: (0, 0)),
    ] + ([] if came is None else [third])
    return pl.pallas_call(
        functools.partial(weight_grads_kernel, came is not None),
        grid_spec=pltpu.PrefetchScalarGridSpec(
            num_scalar_prefetch=1, grid=(3,), in_specs=specs, out_specs=third
        ),
        out_shape=jax.ShapeDtypeStruct((size, 3 * hid), BF16),
        cost_estimate=pl.CostEstimate(
            flops=6 * whole * size * hid,
            bytes_accessed=4 * whole * size + 6 * whole * hid + 6 * size * hid,
            transcendentals=0,
        ),
        name="weight_grads",
    )(jnp.full((1,), quarter, jnp.int32), *inputs)


def picks(targets, slots):
    rows = lax.broadcasted_iota(jnp.int32, (slots, targets.shape[1]), 0)
    return [rows == targets[k : k + 1, :] for k in range(2)]


def combine_kernel(spots, targets, gates, b0, b1, b2, b3, cotangent, out, grad_gates, back):
    for turn, block in enumerate((b0, b1, b2, b3)):
        for j in range(16):
            back[turn * 128 : (turn + 1) * 128, block_cols(j)] = block[:, spot(spots, turn, j)]
    tokens = out.shape[0]
    first, second = [
        jnp.where(hit, 1.0, 0.0).astype(BF16) for hit in picks(targets[...], back.shape[0])
    ]
    g0, g1 = gates[:, 0:1], gates[:, 1:2]
    s0 = jnp.zeros((tokens, LANES), F32)
    s1 = jnp.zeros((tokens, LANES), F32)
    for j in range(4):
        cols = slice(j * 512, (j + 1) * 512)
        o0 = lax.dot_general(first, back[:, cols], TN, preferred_element_type=F32)
        o1 = lax.dot_general(second, back[:, cols], TN, preferred_element_type=F32)
        out[:, cols] = (g0 * o0 + g1 * o1).astype(BF16)
        dy = cotangent[:, cols].astype(F32)
        t0, t1 = o0 * dy, o1 * dy
        for i in range(4):
            s0 = s0 + t0[:, block_cols(i)]
            s1 = s1 + t1[:, block_cols(i)]
    grad_gates[:, 0:1] = jnp.sum(s0, axis=1, keepdims=True)
    grad_gates[:, 1:2] = jnp.sum(s1, axis=1, keepdims=True)


def combine(spots, targets, gates, blocks, cotangent):
    (rows, width), slots = cotangent.shape, 4 * blocks[0].shape[0]
    return pl.pallas_call(
        combine_kernel,
        out_shape=[
            jax.ShapeDtypeStruct((rows, width), BF16),
            jax.ShapeDtypeStruct(gates.shape, F32),
        ],
        in_specs=[SMEM] + [VMEM] * 7,
        out_specs=[VMEM] * 2,
        scratch_shapes=[pltpu.VMEM((slots, width), BF16)],
        cost_estimate=pl.CostEstimate(
            flops=4 * slots * rows * width, bytes_accessed=2 * slots * width * 2, transcendentals=0
        ),
        name="combine",
    )(spots, targets, gates, *blocks, cotangent)


def grad_tokens_kernel(spots, targets, b0, b1, b2, b3, out, back):
    cap = b0.shape[0] // 4
    for step, block in enumerate((b0, b1, b2, b3)):
        for turn in range(4):
            row = (turn * 4 + step) * cap
            for j in range(16):
                back[row : row + cap, block_cols(j)] = block[
                    turn * cap : (turn + 1) * cap, spot(spots, turn, j)
                ]
    hits = picks(targets[...], back.shape[0])
    pick = jnp.where(hits[0] | hits[1], 1.0, 0.0).astype(BF16)
    for j in range(4):
        cols = slice(j * 512, (j + 1) * 512)
        out[:, cols] = lax.dot_general(
            pick, back[:, cols], TN, preferred_element_type=F32
        ).astype(BF16)


def combine_grads(spots, targets, blocks):
    width, slots, rows = blocks[0].shape[1], 4 * blocks[0].shape[0], targets.shape[1]
    return pl.pallas_call(
        grad_tokens_kernel,
        out_shape=jax.ShapeDtypeStruct((rows, width), BF16),
        in_specs=[SMEM] + [VMEM] * 5,
        out_specs=VMEM,
        scratch_shapes=[pltpu.VMEM((slots, width), BF16)],
        cost_estimate=pl.CostEstimate(
            flops=2 * slots * rows * width, bytes_accessed=2 * slots * width * 2, transcendentals=0
        ),
        name="grad_tokens",
    )(spots, targets, *blocks)


def over_z(mover, blocks):
    return [blocks[0]] + [mover(blocks[turn], turn) for turn in range(1, 4)]


def over_y(sign, blocks):
    return [blocks[0]] + [y_send(blocks[dy], sign * dy) for dy in range(1, 4)]


def shards(tokens, routes, gates, cotangent, w_gate, w_up, w_down):
    hid = w_gate.shape[2]
    spots = column_spots()
    routes_t, gates_t = routes.T, gates.T

    own = jnp.concatenate([w_gate[0], w_up[0], w_down[0].T], axis=1)
    far = push(own, dz=1)

    *x_sent, targets = send(True, spots, routes_t, gates_t, tokens)
    x_met = over_z(z_send, x_sent)
    d_sent = send(False, spots, routes_t, gates_t, cotangent)
    d_met = over_y(1, d_sent)

    first = over_x(jnp.concatenate([own] * 4, axis=0))
    second = over_x(jnp.concatenate([far] * 4, axis=0))
    first_other = push(first, dc=1)
    second_other = push(second, dc=1)
    quarters = first, second, first_other, second_other

    d_met = turn_blocks(d_met)
    d_blocks = over_z(z_send, d_met)
    x_met = turn_blocks(x_met)
    x_blocks = over_y(1, x_met)

    x_in, hidden, act, slope, *o_sent = forward(x_blocks, quarters, hid)
    o_met = over_y(-1, o_sent)
    d_in, d_both = hidden_grads(d_blocks, quarters, act, slope)
    saved = x_in, d_in, d_both, hidden

    came1 = weight_grads(3, *saved)
    came1 = push(came1, dc=1)
    came0 = weight_grads(2, *saved)
    came0 = push(came0, dc=1)

    def sum_over_x(dz, came):
        both = weight_grads(dz, *saved, came)
        met = over_x(both)
        return add(*[met[block_cols(i)] for i in range(4)])

    far_sum = sum_over_x(1, came1).astype(BF16)
    far_sum = push(far_sum, dz=1)
    r_sent = row_grads(d_both, quarters)
    r_met = over_z(z_return, r_sent)
    grads = add(sum_over_x(0, came0), far_sum).astype(BF16)

    o_met = turn_blocks(o_met)
    o_blocks = over_z(z_return, o_met)
    r_met = turn_blocks(r_met)
    r_blocks = over_y(-1, r_met)
    output, grad_gates = combine(spots, targets, gates, o_blocks, cotangent)
    grad_tokens = combine_grads(spots, targets, r_blocks)
    return (
        output,
        grad_tokens,
        grad_gates,
        grads[None, :, :hid],
        grads[None, :, hid : 2 * hid],
        grads[:, 2 * hid :].T[None],
    )


def solution(mesh):
    return jax.shard_map(
        shards,
        mesh=mesh,
        in_specs=(
            P(("dp", "expert"), None),
            P(("dp", "expert"), None),
            P(("dp", "expert"), None),
            P(("dp", "expert"), None),
            P("expert", "dp", None),
            P("expert", "dp", None),
            P("expert", None, "dp"),
        ),
        out_specs=(
            P(("dp", "expert"), None),
            P(("dp", "expert"), None),
            P(("dp", "expert"), None),
            P("expert", "dp", None),
            P("expert", "dp", None),
            P("expert", None, "dp"),
        ),
        check_vma=False,
    )
```

```python
import functools

import jax
import jax.numpy as jnp
import numpy as np
from jax import lax
from jax.experimental import pallas as pl
from jax.experimental.pallas import tpu as pltpu
from jax.sharding import PartitionSpec as P

LANES = 128
F32 = jnp.float32
BF16 = jnp.bfloat16
VMEM = pl.BlockSpec(memory_space=pltpu.VMEM)
SMEM = pl.BlockSpec(memory_space=pltpu.SMEM)


def neighbour(i, dx, dz, dc):
    z, x, c = i // 8, i // 2 % 4, i % 2
    return ((z ^ dz) * 4 + (x + dx) % 4) * 2 + (c ^ dc)


BLOCKS = [(dc, dz, dx) for dc in range(2) for dz in range(2) for dx in range(4)]


def push(value, dx=0, dz=0, dc=0):
    return lax.ppermute(value, "dp", [(i, neighbour(i, dx, dz, dc)) for i in range(16)])


def z_target(dp, expert, turn):
    shift = (0, 1, -2 if dp % 2 else 2, -1)[turn]
    z = (dp // 8 * 4 + expert % 4 + shift) % 8
    return z // 4 * 8 + dp % 8, expert // 4 * 4 + z % 4


def z_pairs(turn):
    pairs = []
    for i in range(256):
        dp, expert = z_target(i // 16, i % 16, turn)
        pairs.append((i, dp * 16 + expert))
    return pairs


def z_send(value, turn):
    return lax.ppermute(value, ("dp", "expert"), z_pairs(turn))


def z_return(value, turn):
    return lax.ppermute(value, ("dp", "expert"), [(j, i) for i, j in z_pairs(turn)])


def y_send(value, dy):
    return lax.ppermute(value, "expert", [(i, (i + 4 * dy) % 16) for i in range(16)])


def column_spots():
    spots = np.zeros((16, 16), np.int32)
    for i in range(16):
        for j, block in enumerate(BLOCKS):
            spots[i, neighbour(i, *reversed(block))] = j
    table = np.zeros((256, 4, 16), np.int32)
    for i in range(256):
        for turn in range(4):
            table[i, turn] = spots[z_target(i // 16, i % 16, turn)[0]]
    return jnp.array(table)[lax.axis_index("dp") * 16 + lax.axis_index("expert")]


def add(*values):
    total = values[0].astype(F32)
    for value in values[1:]:
        total = total + value.astype(F32)
    return total


def block_cols(j):
    return slice(j * LANES, (j + 1) * LANES)


def spot(spots, turn, j):
    return pl.ds(pl.multiple_of(spots[turn, j] * LANES, LANES), LANES)


def place_in_buffer(me, cap, experts, routes):
    tokens = routes.shape[1]
    lanes = [routes[k : k + 1, :] for k in range(2)]
    kinds = lax.broadcasted_iota(jnp.int32, (experts, tokens), 0)
    hits = [(kinds == lane).astype(F32) for lane in lanes]
    earlier = lax.broadcasted_iota(jnp.int32, (tokens, tokens), 0) < lax.broadcasted_iota(
        jnp.int32, (tokens, tokens), 1
    )
    counts = jnp.dot(
        (hits[0] + hits[1]).astype(BF16),
        earlier.astype(F32).astype(BF16),
        preferred_element_type=F32,
    )
    targets = []
    for k in range(2):
        slot = jnp.sum(counts * hits[k], axis=0, keepdims=True).astype(jnp.int32)
        turns, steps = (lanes[k] - me) & 3, ((lanes[k] >> 2) - (me >> 2)) & 3
        targets.append((turns * 4 + steps) * cap + slot)
    return targets


def send_kernel(scaled, cap, experts, spots, me, routes, gates, rows, *outs):
    targets = place_in_buffer(me[0], cap, experts, routes[...])
    spots_of = lax.broadcasted_iota(jnp.int32, (experts * cap, rows.shape[0]), 0)
    hits = [spots_of == target for target in targets]
    pick = jnp.where(hits[0] | hits[1], 1.0, 0.0).astype(BF16)
    if scaled:
        weight = jnp.where(hits[0], gates[0:1, :], 0.0) + jnp.where(hits[1], gates[1:2, :], 0.0)
        row_gate = jnp.sum(weight, axis=1, keepdims=True)
    else:
        outs[4][0:1, :], outs[4][1:2, :] = targets
    for j in range(4):
        moved = jnp.dot(pick, rows[:, j * 512 : (j + 1) * 512], preferred_element_type=F32)
        if scaled:
            moved = moved * row_gate
        moved = moved.astype(BF16)
        for i in range(4):
            for turn in range(4):
                cols = spot(spots, turn, j * 4 + i)
                for step in range(4):
                    row = (turn * 4 + step) * cap
                    outs[step][turn * cap : (turn + 1) * cap, cols] = moved[
                        row : row + cap, block_cols(i)
                    ]


def send(scaled, spots, routes, gates, rows):
    (tokens, width), experts = rows.shape, lax.axis_size("expert")
    cap = tokens * routes.shape[0] * 2 // experts
    slots = experts * cap
    shapes = [jax.ShapeDtypeStruct((slots // 4, width), BF16)] * 4
    if not scaled:
        shapes = shapes + [jax.ShapeDtypeStruct(routes.shape, jnp.int32)]
    return pl.pallas_call(
        functools.partial(send_kernel, scaled, cap, experts),
        out_shape=shapes,
        in_specs=[SMEM] * 2 + [VMEM] * 3,
        out_specs=[VMEM] * len(shapes),
        cost_estimate=pl.CostEstimate(
            flops=2 * slots * tokens * width, bytes_accessed=3 * slots * width, transcendentals=0
        ),
        name="send",
    )(spots, lax.axis_index("expert").reshape(1), routes, gates, rows)


def turn_kernel(b0, b1, b2, b3, *outs):
    size = b0.shape[0] // 4
    for i, block in enumerate((b0, b1, b2, b3)):
        for k in range(4):
            outs[k][i * size : (i + 1) * size] = block[k * size : (k + 1) * size]


def turn_blocks(blocks):
    return pl.pallas_call(
        turn_kernel,
        out_shape=[jax.ShapeDtypeStruct(blocks[0].shape, BF16)] * 4,
        in_specs=[VMEM] * 4,
        out_specs=[VMEM] * 4,
        cost_estimate=pl.CostEstimate(
            flops=0, bytes_accessed=16 * blocks[0].size, transcendentals=0
        ),
        name="turn",
    )(*blocks)


NT = (((1,), (1,)), ((), ()))
TN = (((0,), (0,)), ((), ()))


def chunk(n, size):
    return pl.ds(pl.multiple_of(n * size, size), size)


def quarter_dot(a, quarters, where):
    depth = quarters[0].shape[0]
    total = None
    for q, w in enumerate(quarters):
        part = jnp.dot(
            a[:, q * depth : (q + 1) * depth], w[:, where], preferred_element_type=F32
        )
        total = part if total is None else total + part
    return total


def forward_kernel(b0, b1, b2, b3, w0, w1, w2, w3, x_in, hidden, act, slope, *outs):
    size, hid = b0.shape[0], hidden.shape[1]
    quarters = (w0, w1, w2, w3)
    for k, block in enumerate((b0, b1, b2, b3)):
        x_in[k * size : (k + 1) * size] = block[...]

    @pl.loop(0, hid // 256)
    def _(n):
        cols, up_cols = chunk(n, 256), pl.ds(pl.multiple_of(hid + n * 256, 256), 256)
        pre, up = quarter_dot(x_in, quarters, cols), quarter_dot(x_in, quarters, up_cols)
        sig = jax.nn.sigmoid(pre)
        silu = pre * sig
        act[:, cols] = silu.astype(BF16)
        slope[:, cols] = (up * sig * (1.0 + pre * (1.0 - sig))).astype(BF16)
        hidden[:, cols] = (silu * up).astype(BF16)

    for q, w in enumerate(quarters):
        rows = lax.dot_general(
            hidden[...], w[:, 2 * hid :], NT, preferred_element_type=F32
        ).astype(BF16)
        for k in range(4):
            outs[k][:, q * 512 : (q + 1) * 512] = rows[k * size : (k + 1) * size]


def forward(blocks, quarters, hid):
    rows, width = blocks[0].shape
    whole = 4 * rows
    return pl.pallas_call(
        forward_kernel,
        out_shape=[jax.ShapeDtypeStruct((whole, width), BF16)]
        + [jax.ShapeDtypeStruct((whole, hid), BF16)] * 3
        + [jax.ShapeDtypeStruct((rows, width), BF16)] * 4,
        in_specs=[VMEM] * 8,
        out_specs=[VMEM] * 8,
        cost_estimate=pl.CostEstimate(
            flops=6 * whole * width * hid,
            bytes_accessed=6 * width * hid + 6 * whole * width + 6 * whole * hid,
            transcendentals=whole * hid,
        ),
        name="forward",
    )(*blocks, *quarters)


def hidden_kernel(b0, b1, b2, b3, w0, w1, w2, w3, act, slope, d_in, d_both):
    size, hid = b0.shape[0], act.shape[1]
    for k, block in enumerate((b0, b1, b2, b3)):
        d_in[k * size : (k + 1) * size] = block[...]

    @pl.loop(0, hid // 256)
    def _(n):
        cols, up_cols = chunk(n, 256), pl.ds(pl.multiple_of(hid + n * 256, 256), 256)
        d_hidden = quarter_dot(d_in, (w0, w1, w2, w3), cols)
        d_both[:, cols] = (d_hidden * slope[:, cols].astype(F32)).astype(BF16)
        d_both[:, up_cols] = (d_hidden * act[:, cols].astype(F32)).astype(BF16)


def whole_spec(shape):
    return pl.BlockSpec(shape, lambda *_: (0,) * len(shape))


def hidden_grads(blocks, quarters, act, slope):
    (rows, width), (whole, hid) = blocks[0].shape, act.shape
    return pl.pallas_call(
        hidden_kernel,
        grid=(1,),
        out_shape=[
            jax.ShapeDtypeStruct((whole, width), BF16),
            jax.ShapeDtypeStruct((whole, 2 * hid), BF16),
        ],
        in_specs=[whole_spec((rows, width))] * 4
        + [pl.BlockSpec((width // 4, hid), lambda i: (0, 2))] * 4
        + [whole_spec((whole, hid))] * 2,
        out_specs=[whole_spec((whole, width)), whole_spec((whole, 2 * hid))],
        cost_estimate=pl.CostEstimate(
            flops=2 * whole * width * hid,
            bytes_accessed=2 * width * hid + 4 * whole * width + 8 * whole * hid,
            transcendentals=0,
        ),
        name="hidden_grads",
    )(*blocks, *quarters, act, slope)


def row_grads_kernel(d_both, w0, w1, w2, w3, *outs):
    size = outs[0].shape[0]
    for q, w in enumerate((w0, w1, w2, w3)):
        rows = lax.dot_general(d_both[...], w[...], NT, preferred_element_type=F32).astype(BF16)
        for k in range(4):
            outs[k][:, q * 512 : (q + 1) * 512] = rows[k * size : (k + 1) * size]


def row_grads(d_both, quarters):
    (whole, both), width = d_both.shape, 4 * quarters[0].shape[0]
    return pl.pallas_call(
        row_grads_kernel,
        grid=(1,),
        out_shape=[jax.ShapeDtypeStruct((whole // 4, width), BF16)] * 4,
        in_specs=[whole_spec((whole, both))]
        + [pl.BlockSpec((width // 4, both), lambda i: (0, 0))] * 4,
        out_specs=[whole_spec((whole // 4, width))] * 4,
        cost_estimate=pl.CostEstimate(
            flops=2 * whole * width * both,
            bytes_accessed=2 * (width * both + whole * width + whole * both),
            transcendentals=0,
        ),
        name="row_grads",
    )(d_both, *quarters)


def weight_grads_kernel(base, x_in, d_in, d_both, hidden, *refs):
    def put(value):
        if len(refs) == 1:
            refs[0][...] = value.astype(BF16)
        else:
            value = (value + refs[0][...].astype(F32)).astype(BF16)
            for i, out in enumerate(refs[1:]):
                out[...] = value[i * LANES : (i + 1) * LANES]

    @pl.when(pl.program_id(0) < 2)
    def _():
        put(lax.dot_general(x_in[...], d_both[...], TN, preferred_element_type=F32))

    @pl.when(pl.program_id(0) == 2)
    def _():
        put(lax.dot_general(d_in[...], hidden[...], TN, preferred_element_type=F32))


def weight_grads(quarter, x_in, d_in, d_both, hidden, came=None):
    (whole, width), hid = x_in.shape, hidden.shape[1]
    size = width // 4
    columns = pl.BlockSpec((whole, size), lambda n, base: (0, base[0]))
    third = pl.BlockSpec((size, hid), lambda n, base: (0, n))
    inputs = [x_in, d_in, d_both, hidden]
    specs = [
        columns,
        columns,
        pl.BlockSpec((whole, hid), lambda n, base: (0, jnp.minimum(n, 1))),
        pl.BlockSpec((whole, hid), lambda n, base: (0, 0)),
    ]
    shape, out = jax.ShapeDtypeStruct((size, 3 * hid), BF16), third
    if came is not None:
        inputs, specs = inputs + [came], specs + [third]
        shape = [jax.ShapeDtypeStruct((LANES, 3 * hid), BF16)] * 4
        out = [pl.BlockSpec((LANES, hid), lambda n, base: (0, n))] * 4
    return pl.pallas_call(
        weight_grads_kernel,
        grid_spec=pltpu.PrefetchScalarGridSpec(
            num_scalar_prefetch=1, grid=(3,), in_specs=specs, out_specs=out
        ),
        out_shape=shape,
        cost_estimate=pl.CostEstimate(
            flops=6 * whole * size * hid,
            bytes_accessed=4 * whole * size + 6 * whole * hid + 6 * size * hid,
            transcendentals=0,
        ),
        name="weight_grads",
    )(jnp.full((1,), quarter, jnp.int32), *inputs)


def picks(targets, slots):
    rows = lax.broadcasted_iota(jnp.int32, (slots, targets.shape[1]), 0)
    return [rows == targets[k : k + 1, :] for k in range(2)]


def gather_back(spots, blocks, back):
    cap = blocks[0].shape[0] // 4
    for step, block in enumerate(blocks):
        for turn in range(4):
            row = (turn * 4 + step) * cap
            for j in range(16):
                back[row : row + cap, block_cols(j)] = block[
                    turn * cap : (turn + 1) * cap, spot(spots, turn, j)
                ]


def combine_kernel(spots, targets, gates, b0, b1, b2, b3, cotangent, out, grad_gates, back):
    gather_back(spots, (b0, b1, b2, b3), back)
    tokens = out.shape[0]
    first, second = [
        jnp.where(hit, 1.0, 0.0).astype(BF16) for hit in picks(targets[...], back.shape[0])
    ]
    g0, g1 = gates[:, 0:1], gates[:, 1:2]
    s0 = jnp.zeros((tokens, LANES), F32)
    s1 = jnp.zeros((tokens, LANES), F32)
    for j in range(4):
        cols = slice(j * 512, (j + 1) * 512)
        o0 = lax.dot_general(first, back[:, cols], TN, preferred_element_type=F32)
        o1 = lax.dot_general(second, back[:, cols], TN, preferred_element_type=F32)
        out[:, cols] = (g0 * o0 + g1 * o1).astype(BF16)
        dy = cotangent[:, cols].astype(F32)
        t0, t1 = o0 * dy, o1 * dy
        for i in range(4):
            s0 = s0 + t0[:, block_cols(i)]
            s1 = s1 + t1[:, block_cols(i)]
    grad_gates[:, 0:1] = jnp.sum(s0, axis=1, keepdims=True)
    grad_gates[:, 1:2] = jnp.sum(s1, axis=1, keepdims=True)


def combine(spots, targets, gates, blocks, cotangent):
    (rows, width), slots = cotangent.shape, 4 * blocks[0].shape[0]
    return pl.pallas_call(
        combine_kernel,
        out_shape=[
            jax.ShapeDtypeStruct((rows, width), BF16),
            jax.ShapeDtypeStruct(gates.shape, F32),
        ],
        in_specs=[SMEM] + [VMEM] * 7,
        out_specs=[VMEM] * 2,
        scratch_shapes=[pltpu.VMEM((slots, width), BF16)],
        cost_estimate=pl.CostEstimate(
            flops=4 * slots * rows * width, bytes_accessed=2 * slots * width * 2, transcendentals=0
        ),
        name="combine",
    )(spots, targets, gates, *blocks, cotangent)


def grad_tokens_kernel(spots, targets, b0, b1, b2, b3, out, back):
    gather_back(spots, (b0, b1, b2, b3), back)
    hits = picks(targets[...], back.shape[0])
    pick = jnp.where(hits[0] | hits[1], 1.0, 0.0).astype(BF16)
    for j in range(4):
        cols = slice(j * 512, (j + 1) * 512)
        out[:, cols] = lax.dot_general(
            pick, back[:, cols], TN, preferred_element_type=F32
        ).astype(BF16)


def combine_grads(spots, targets, blocks):
    width, slots, rows = blocks[0].shape[1], 4 * blocks[0].shape[0], targets.shape[1]
    return pl.pallas_call(
        grad_tokens_kernel,
        out_shape=jax.ShapeDtypeStruct((rows, width), BF16),
        in_specs=[SMEM] + [VMEM] * 5,
        out_specs=VMEM,
        scratch_shapes=[pltpu.VMEM((slots, width), BF16)],
        cost_estimate=pl.CostEstimate(
            flops=2 * slots * rows * width, bytes_accessed=2 * slots * width * 2, transcendentals=0
        ),
        name="grad_tokens",
    )(spots, targets, *blocks)


def over_z(mover, blocks):
    return [blocks[0]] + [mover(blocks[turn], turn) for turn in range(1, 4)]


def over_x(block):
    return jnp.concatenate([block] + [push(block, dx=-dx) for dx in (1, 2, 3)], axis=0)


def over_y(sign, blocks):
    return [blocks[0]] + [y_send(blocks[dy], sign * dy) for dy in range(1, 4)]


def shards(tokens, routes, gates, cotangent, w_gate, w_up, w_down):
    hid = w_gate.shape[2]
    spots = column_spots()
    routes_t, gates_t = routes.T, gates.T

    own = jnp.concatenate([w_gate[0], w_up[0], w_down[0].T], axis=1)
    far = push(own, dz=1)

    *x_met, targets = send(False, spots, routes_t, gates_t, tokens)
    x_met = over_y(1, x_met)
    d_met = send(True, spots, routes_t, gates_t, cotangent)
    d_met = over_y(1, d_met)

    first = over_x(own)
    second = over_x(far)
    first_other = push(first, dc=1)
    second_other = push(second, dc=1)
    quarters = first, second, first_other, second_other

    x_met = turn_blocks(x_met)
    x_blocks = over_z(z_send, x_met)
    d_met = turn_blocks(d_met)
    d_blocks = over_z(z_send, d_met)

    x_in, hidden, act, slope, *o_sent = forward(x_blocks, quarters, hid)
    o_met = over_z(z_return, o_sent)
    d_in, d_both = hidden_grads(d_blocks, quarters, act, slope)
    saved = x_in, d_in, d_both, hidden

    came1 = weight_grads(3, *saved)
    came1 = push(came1, dc=1)
    came0 = weight_grads(2, *saved)
    came0 = push(came0, dc=1)

    def sum_over_x(dz, came):
        mine, *rest = weight_grads(dz, *saved, came)
        met = [push(rest[dx - 1], dx=dx) for dx in (1, 2, 3)]
        return add(mine, *met)

    far_sum = sum_over_x(1, came1).astype(BF16)
    far_sum = push(far_sum, dz=1)
    r_sent = row_grads(d_both, quarters)
    r_met = over_z(z_return, r_sent)
    grads = add(sum_over_x(0, came0), far_sum).astype(BF16)

    o_met = turn_blocks(o_met)
    o_blocks = over_y(-1, o_met)
    r_met = turn_blocks(r_met)
    r_blocks = over_y(-1, r_met)
    output, grad_gates = combine(spots, targets, gates, o_blocks, cotangent)
    grad_tokens = combine_grads(spots, targets, r_blocks)
    return (
        output,
        grad_tokens,
        grad_gates,
        grads[None, :, :hid],
        grads[None, :, hid : 2 * hid],
        grads[:, 2 * hid :].T[None],
    )


def solution(mesh):
    return jax.shard_map(
        shards,
        mesh=mesh,
        in_specs=(
            P(("dp", "expert"), None),
            P(("dp", "expert"), None),
            P(("dp", "expert"), None),
            P(("dp", "expert"), None),
            P("expert", "dp", None),
            P("expert", "dp", None),
            P("expert", None, "dp"),
        ),
        out_specs=(
            P(("dp", "expert"), None),
            P(("dp", "expert"), None),
            P(("dp", "expert"), None),
            P("expert", "dp", None),
            P("expert", "dp", None),
            P("expert", None, "dp"),
        ),
        check_vma=False,
    )
```

```python
import functools

import jax
import jax.numpy as jnp
import numpy as np
from jax import lax
from jax.experimental import pallas as pl
from jax.experimental.pallas import tpu as pltpu
from jax.sharding import PartitionSpec as P

LANES = 128
F32 = jnp.float32
BF16 = jnp.bfloat16
VMEM = pl.BlockSpec(memory_space=pltpu.VMEM)
SMEM = pl.BlockSpec(memory_space=pltpu.SMEM)


def grant(mib):
    return pltpu.CompilerParams(vmem_limit_bytes=mib << 20)


def neighbour(i, dx, dz, dc):
    z, x, c = i // 8, i // 2 % 4, i % 2
    return ((z ^ dz) * 4 + (x + dx) % 4) * 2 + (c ^ dc)


BLOCKS = [(dc, dz, dx) for dc in range(2) for dz in range(2) for dx in range(4)]


def push(value, dx=0, dz=0, dc=0):
    return lax.ppermute(value, "dp", [(i, neighbour(i, dx, dz, dc)) for i in range(16)])


def z_target(dp, expert, turn):
    shift = (0, 1, -2 if dp % 2 else 2, -1)[turn]
    z = (dp // 8 * 4 + expert % 4 + shift) % 8
    return z // 4 * 8 + dp % 8, expert // 4 * 4 + z % 4


def z_pairs(turn):
    pairs = []
    for i in range(256):
        dp, expert = z_target(i // 16, i % 16, turn)
        pairs.append((i, dp * 16 + expert))
    return pairs


def z_send(value, turn):
    return lax.ppermute(value, ("dp", "expert"), z_pairs(turn))


def z_return(value, turn):
    return lax.ppermute(value, ("dp", "expert"), [(j, i) for i, j in z_pairs(turn)])


def y_send(value, dy):
    return lax.ppermute(value, "expert", [(i, (i + 4 * dy) % 16) for i in range(16)])


def column_spots():
    spots = np.zeros((16, 16), np.int32)
    for i in range(16):
        for j, block in enumerate(BLOCKS):
            spots[i, neighbour(i, *reversed(block))] = j
    table = np.zeros((256, 4, 16), np.int32)
    for i in range(256):
        for turn in range(4):
            table[i, turn] = spots[z_target(i // 16, i % 16, turn)[0]]
    return jnp.array(table)[lax.axis_index("dp") * 16 + lax.axis_index("expert")]


def add(*values):
    total = values[0].astype(F32)
    for value in values[1:]:
        total = total + value.astype(F32)
    return total


def block_cols(j):
    return slice(j * LANES, (j + 1) * LANES)


def spot(spots, turn, j):
    return pl.ds(pl.multiple_of(spots[turn, j] * LANES, LANES), LANES)


def place_in_buffer(me, cap, experts, routes):
    tokens = routes.shape[1]
    lanes = [routes[k : k + 1, :] for k in range(2)]
    kinds = lax.broadcasted_iota(jnp.int32, (experts, tokens), 0)
    hits = [(kinds == lane).astype(F32) for lane in lanes]
    earlier = lax.broadcasted_iota(jnp.int32, (tokens, tokens), 0) < lax.broadcasted_iota(
        jnp.int32, (tokens, tokens), 1
    )
    counts = jnp.dot(
        (hits[0] + hits[1]).astype(BF16),
        earlier.astype(F32).astype(BF16),
        preferred_element_type=F32,
    )
    targets = []
    for k in range(2):
        slot = jnp.sum(counts * hits[k], axis=0, keepdims=True).astype(jnp.int32)
        turns, steps = (lanes[k] - me) & 3, ((lanes[k] >> 2) - (me >> 2)) & 3
        targets.append((turns * 4 + steps) * cap + slot)
    return targets


def send_kernel(scaled, cap, experts, spots, me, routes, gates, rows, *outs):
    targets = place_in_buffer(me[0], cap, experts, routes[...])
    spots_of = lax.broadcasted_iota(jnp.int32, (experts * cap, rows.shape[0]), 0)
    hits = [spots_of == target for target in targets]
    pick = jnp.where(hits[0] | hits[1], 1.0, 0.0).astype(BF16)
    if scaled:
        weight = jnp.where(hits[0], gates[0:1, :], 0.0) + jnp.where(hits[1], gates[1:2, :], 0.0)
        row_gate = jnp.sum(weight, axis=1, keepdims=True)
    else:
        outs[4][0:1, :], outs[4][1:2, :] = targets
    for j in range(4):
        moved = jnp.dot(pick, rows[:, j * 512 : (j + 1) * 512], preferred_element_type=F32)
        if scaled:
            moved = moved * row_gate
        moved = moved.astype(BF16)
        for i in range(4):
            for turn in range(4):
                cols = spot(spots, turn, j * 4 + i)
                for step in range(4):
                    row = (turn * 4 + step) * cap
                    outs[step][turn * cap : (turn + 1) * cap, cols] = moved[
                        row : row + cap, block_cols(i)
                    ]


def send(scaled, spots, routes, gates, rows):
    (tokens, width), experts = rows.shape, lax.axis_size("expert")
    cap = tokens * routes.shape[0] * 2 // experts
    slots = experts * cap
    shapes = [jax.ShapeDtypeStruct((slots // 4, width), BF16)] * 4
    if not scaled:
        shapes = shapes + [jax.ShapeDtypeStruct(routes.shape, jnp.int32)]
    return pl.pallas_call(
        functools.partial(send_kernel, scaled, cap, experts),
        out_shape=shapes,
        in_specs=[SMEM] * 2 + [VMEM] * 3,
        out_specs=[VMEM] * len(shapes),
        cost_estimate=pl.CostEstimate(
            flops=2 * slots * tokens * width, bytes_accessed=3 * slots * width, transcendentals=0
        ),
        name="send",
        compiler_params=grant(7),
    )(spots, lax.axis_index("expert").reshape(1), routes, gates, rows)


def turn_kernel(b0, b1, b2, b3, *outs):
    size = b0.shape[0] // 4
    for i, block in enumerate((b0, b1, b2, b3)):
        for k in range(4):
            outs[k][i * size : (i + 1) * size] = block[k * size : (k + 1) * size]


def turn_blocks(blocks):
    return pl.pallas_call(
        turn_kernel,
        out_shape=[jax.ShapeDtypeStruct(blocks[0].shape, BF16)] * 4,
        in_specs=[VMEM] * 4,
        out_specs=[VMEM] * 4,
        cost_estimate=pl.CostEstimate(
            flops=0, bytes_accessed=16 * blocks[0].size, transcendentals=0
        ),
        name="turn",
        compiler_params=grant(6),
    )(*blocks)


NT = (((1,), (1,)), ((), ()))
TN = (((0,), (0,)), ((), ()))


def chunk(n, size):
    return pl.ds(pl.multiple_of(n * size, size), size)


def quarter_dot(a, quarters, where):
    depth = quarters[0].shape[0]
    total = None
    for q, w in enumerate(quarters):
        part = jnp.dot(
            a[:, q * depth : (q + 1) * depth], w[:, where], preferred_element_type=F32
        )
        total = part if total is None else total + part
    return total


def forward_kernel(b0, b1, b2, b3, w0, w1, w2, w3, x_in, hidden, act, slope, *outs):
    size, hid = b0.shape[0], hidden.shape[1]
    quarters = (w0, w1, w2, w3)
    for k, block in enumerate((b0, b1, b2, b3)):
        x_in[k * size : (k + 1) * size] = block[...]

    @pl.loop(0, hid // 256)
    def _(n):
        cols, up_cols = chunk(n, 256), pl.ds(pl.multiple_of(hid + n * 256, 256), 256)
        pre, up = quarter_dot(x_in, quarters, cols), quarter_dot(x_in, quarters, up_cols)
        sig = jax.nn.sigmoid(pre)
        silu = pre * sig
        act[:, cols] = silu.astype(BF16)
        slope[:, cols] = (up * sig * (1.0 + pre * (1.0 - sig))).astype(BF16)
        hidden[:, cols] = (silu * up).astype(BF16)

    for q, w in enumerate(quarters):
        rows = lax.dot_general(
            hidden[...], w[:, 2 * hid :], NT, preferred_element_type=F32
        ).astype(BF16)
        for k in range(4):
            outs[k][:, q * 512 : (q + 1) * 512] = rows[k * size : (k + 1) * size]


def forward(blocks, quarters, hid):
    rows, width = blocks[0].shape
    whole = 4 * rows
    return pl.pallas_call(
        forward_kernel,
        out_shape=[jax.ShapeDtypeStruct((whole, width), BF16)]
        + [jax.ShapeDtypeStruct((whole, hid), BF16)] * 3
        + [jax.ShapeDtypeStruct((rows, width), BF16)] * 4,
        in_specs=[VMEM] * 8,
        out_specs=[VMEM] * 8,
        cost_estimate=pl.CostEstimate(
            flops=6 * whole * width * hid,
            bytes_accessed=6 * width * hid + 6 * whole * width + 6 * whole * hid,
            transcendentals=whole * hid,
        ),
        name="forward",
        compiler_params=grant(22),
    )(*blocks, *quarters)


def hidden_kernel(b0, b1, b2, b3, w0, w1, w2, w3, act, slope, d_in, d_both):
    size, hid = b0.shape[0], act.shape[1]
    for k, block in enumerate((b0, b1, b2, b3)):
        d_in[k * size : (k + 1) * size] = block[...]

    @pl.loop(0, hid // 256)
    def _(n):
        cols, up_cols = chunk(n, 256), pl.ds(pl.multiple_of(hid + n * 256, 256), 256)
        d_hidden = quarter_dot(d_in, (w0, w1, w2, w3), cols)
        d_both[:, cols] = (d_hidden * slope[:, cols].astype(F32)).astype(BF16)
        d_both[:, up_cols] = (d_hidden * act[:, cols].astype(F32)).astype(BF16)


def whole_spec(shape):
    return pl.BlockSpec(shape, lambda *_: (0,) * len(shape))


def hidden_grads(blocks, quarters, act, slope):
    (rows, width), (whole, hid) = blocks[0].shape, act.shape
    return pl.pallas_call(
        hidden_kernel,
        grid=(1,),
        out_shape=[
            jax.ShapeDtypeStruct((whole, width), BF16),
            jax.ShapeDtypeStruct((whole, 2 * hid), BF16),
        ],
        in_specs=[whole_spec((rows, width))] * 4
        + [pl.BlockSpec((width // 4, hid), lambda i: (0, 2))] * 4
        + [whole_spec((whole, hid))] * 2,
        out_specs=[whole_spec((whole, width)), whole_spec((whole, 2 * hid))],
        cost_estimate=pl.CostEstimate(
            flops=2 * whole * width * hid,
            bytes_accessed=2 * width * hid + 4 * whole * width + 8 * whole * hid,
            transcendentals=0,
        ),
        name="hidden_grads",
        compiler_params=grant(14),
    )(*blocks, *quarters, act, slope)


def row_grads_kernel(d_both, w0, w1, w2, w3, *outs):
    size = outs[0].shape[0]
    for q, w in enumerate((w0, w1, w2, w3)):
        rows = lax.dot_general(d_both[...], w[...], NT, preferred_element_type=F32).astype(BF16)
        for k in range(4):
            outs[k][:, q * 512 : (q + 1) * 512] = rows[k * size : (k + 1) * size]


def row_grads(d_both, quarters):
    (whole, both), width = d_both.shape, 4 * quarters[0].shape[0]
    return pl.pallas_call(
        row_grads_kernel,
        grid=(1,),
        out_shape=[jax.ShapeDtypeStruct((whole // 4, width), BF16)] * 4,
        in_specs=[whole_spec((whole, both))]
        + [pl.BlockSpec((width // 4, both), lambda i: (0, 0))] * 4,
        out_specs=[whole_spec((whole // 4, width))] * 4,
        cost_estimate=pl.CostEstimate(
            flops=2 * whole * width * both,
            bytes_accessed=2 * (width * both + whole * width + whole * both),
            transcendentals=0,
        ),
        name="row_grads",
        compiler_params=grant(13),
    )(d_both, *quarters)


def weight_grads_kernel(base, x_in, d_in, d_both, hidden, *refs):
    def put(value):
        if len(refs) == 1:
            refs[0][...] = value.astype(BF16)
        else:
            value = (value + refs[0][...].astype(F32)).astype(BF16)
            for i, out in enumerate(refs[1:]):
                out[...] = value[i * LANES : (i + 1) * LANES]

    @pl.when(pl.program_id(0) < 2)
    def _():
        put(lax.dot_general(x_in[...], d_both[...], TN, preferred_element_type=F32))

    @pl.when(pl.program_id(0) == 2)
    def _():
        put(lax.dot_general(d_in[...], hidden[...], TN, preferred_element_type=F32))


def weight_grads(quarter, x_in, d_in, d_both, hidden, came=None):
    (whole, width), hid = x_in.shape, hidden.shape[1]
    size = width // 4
    columns = pl.BlockSpec((whole, size), lambda n, base: (0, base[0]))
    third = pl.BlockSpec((size, hid), lambda n, base: (0, n))
    inputs = [x_in, d_in, d_both, hidden]
    specs = [
        columns,
        columns,
        pl.BlockSpec((whole, hid), lambda n, base: (0, jnp.minimum(n, 1))),
        pl.BlockSpec((whole, hid), lambda n, base: (0, 0)),
    ]
    shape, out = jax.ShapeDtypeStruct((size, 3 * hid), BF16), third
    if came is not None:
        inputs, specs = inputs + [came], specs + [third]
        shape = [jax.ShapeDtypeStruct((LANES, 3 * hid), BF16)] * 4
        out = [pl.BlockSpec((LANES, hid), lambda n, base: (0, n))] * 4
    return pl.pallas_call(
        weight_grads_kernel,
        grid_spec=pltpu.PrefetchScalarGridSpec(
            num_scalar_prefetch=1, grid=(3,), in_specs=specs, out_specs=out
        ),
        out_shape=shape,
        cost_estimate=pl.CostEstimate(
            flops=6 * whole * size * hid,
            bytes_accessed=4 * whole * size + 6 * whole * hid + 6 * size * hid,
            transcendentals=0,
        ),
        name="weight_grads",
        compiler_params=grant(10),
    )(jnp.full((1,), quarter, jnp.int32), *inputs)


def picks(targets, slots):
    rows = lax.broadcasted_iota(jnp.int32, (slots, targets.shape[1]), 0)
    return [rows == targets[k : k + 1, :] for k in range(2)]


def gather_back(spots, blocks, back):
    cap = blocks[0].shape[0] // 4
    for step, block in enumerate(blocks):
        for turn in range(4):
            row = (turn * 4 + step) * cap
            for j in range(16):
                back[row : row + cap, block_cols(j)] = block[
                    turn * cap : (turn + 1) * cap, spot(spots, turn, j)
                ]


def combine_kernel(spots, targets, gates, b0, b1, b2, b3, cotangent, out, grad_gates, back):
    gather_back(spots, (b0, b1, b2, b3), back)
    tokens = out.shape[0]
    first, second = [
        jnp.where(hit, 1.0, 0.0).astype(BF16) for hit in picks(targets[...], back.shape[0])
    ]
    g0, g1 = gates[:, 0:1], gates[:, 1:2]
    s0 = jnp.zeros((tokens, LANES), F32)
    s1 = jnp.zeros((tokens, LANES), F32)
    for j in range(4):
        cols = slice(j * 512, (j + 1) * 512)
        o0 = lax.dot_general(first, back[:, cols], TN, preferred_element_type=F32)
        o1 = lax.dot_general(second, back[:, cols], TN, preferred_element_type=F32)
        out[:, cols] = (g0 * o0 + g1 * o1).astype(BF16)
        dy = cotangent[:, cols].astype(F32)
        t0, t1 = o0 * dy, o1 * dy
        for i in range(4):
            s0 = s0 + t0[:, block_cols(i)]
            s1 = s1 + t1[:, block_cols(i)]
    grad_gates[:, 0:1] = jnp.sum(s0, axis=1, keepdims=True)
    grad_gates[:, 1:2] = jnp.sum(s1, axis=1, keepdims=True)


def combine(spots, targets, gates, blocks, cotangent):
    (rows, width), slots = cotangent.shape, 4 * blocks[0].shape[0]
    return pl.pallas_call(
        combine_kernel,
        out_shape=[
            jax.ShapeDtypeStruct((rows, width), BF16),
            jax.ShapeDtypeStruct(gates.shape, F32),
        ],
        in_specs=[SMEM] + [VMEM] * 7,
        out_specs=[VMEM] * 2,
        scratch_shapes=[pltpu.VMEM((slots, width), BF16)],
        cost_estimate=pl.CostEstimate(
            flops=4 * slots * rows * width, bytes_accessed=2 * slots * width * 2, transcendentals=0
        ),
        name="combine",
        compiler_params=grant(10),
    )(spots, targets, gates, *blocks, cotangent)


def grad_tokens_kernel(spots, targets, b0, b1, b2, b3, out, back):
    gather_back(spots, (b0, b1, b2, b3), back)
    hits = picks(targets[...], back.shape[0])
    pick = jnp.where(hits[0] | hits[1], 1.0, 0.0).astype(BF16)
    for j in range(4):
        cols = slice(j * 512, (j + 1) * 512)
        out[:, cols] = lax.dot_general(
            pick, back[:, cols], TN, preferred_element_type=F32
        ).astype(BF16)


def combine_grads(spots, targets, blocks):
    width, slots, rows = blocks[0].shape[1], 4 * blocks[0].shape[0], targets.shape[1]
    return pl.pallas_call(
        grad_tokens_kernel,
        out_shape=jax.ShapeDtypeStruct((rows, width), BF16),
        in_specs=[SMEM] + [VMEM] * 5,
        out_specs=VMEM,
        scratch_shapes=[pltpu.VMEM((slots, width), BF16)],
        cost_estimate=pl.CostEstimate(
            flops=2 * slots * rows * width, bytes_accessed=2 * slots * width * 2, transcendentals=0
        ),
        name="grad_tokens",
        compiler_params=grant(8),
    )(spots, targets, *blocks)


def over_z(mover, blocks):
    return [blocks[0]] + [mover(blocks[turn], turn) for turn in range(1, 4)]


def over_x(block):
    return jnp.concatenate([block] + [push(block, dx=-dx) for dx in (1, 2, 3)], axis=0)


def over_y(sign, blocks):
    return [blocks[0]] + [y_send(blocks[dy], sign * dy) for dy in range(1, 4)]


def shards(tokens, routes, gates, cotangent, w_gate, w_up, w_down):
    hid = w_gate.shape[2]
    spots = column_spots()
    routes_t, gates_t = routes.T, gates.T

    own = jnp.concatenate([w_gate[0], w_up[0], w_down[0].T], axis=1)
    far = push(own, dz=1)

    *x_met, targets = send(False, spots, routes_t, gates_t, tokens)
    x_met = over_y(1, x_met)
    d_met = send(True, spots, routes_t, gates_t, cotangent)
    d_met = over_y(1, d_met)

    first = over_x(own)
    second = over_x(far)
    first_other = push(first, dc=1)
    second_other = push(second, dc=1)
    quarters = first, second, first_other, second_other

    x_met = turn_blocks(x_met)
    x_blocks = over_z(z_send, x_met)
    d_met = turn_blocks(d_met)
    d_blocks = over_z(z_send, d_met)

    x_in, hidden, act, slope, *o_sent = forward(x_blocks, quarters, hid)
    o_met = over_z(z_return, o_sent)
    d_in, d_both = hidden_grads(d_blocks, quarters, act, slope)
    saved = x_in, d_in, d_both, hidden

    came1 = weight_grads(3, *saved)
    came1 = push(came1, dc=1)
    came0 = weight_grads(2, *saved)
    came0 = push(came0, dc=1)

    def sum_over_x(dz, came):
        mine, *rest = weight_grads(dz, *saved, came)
        met = [push(rest[dx - 1], dx=dx) for dx in (1, 2, 3)]
        return add(mine, *met)

    far_sum = sum_over_x(1, came1).astype(BF16)
    far_sum = push(far_sum, dz=1)
    r_sent = row_grads(d_both, quarters)
    r_met = over_z(z_return, r_sent)
    grads = add(sum_over_x(0, came0), far_sum).astype(BF16)

    o_met = turn_blocks(o_met)
    o_blocks = over_y(-1, o_met)
    r_met = turn_blocks(r_met)
    r_blocks = over_y(-1, r_met)
    output, grad_gates = combine(spots, targets, gates, o_blocks, cotangent)
    grad_tokens = combine_grads(spots, targets, r_blocks)
    return (
        output,
        grad_tokens,
        grad_gates,
        grads[None, :, :hid],
        grads[None, :, hid : 2 * hid],
        grads[:, 2 * hid :].T[None],
    )


def solution(mesh):
    return jax.shard_map(
        shards,
        mesh=mesh,
        in_specs=(
            P(("dp", "expert"), None),
            P(("dp", "expert"), None),
            P(("dp", "expert"), None),
            P(("dp", "expert"), None),
            P("expert", "dp", None),
            P("expert", "dp", None),
            P("expert", None, "dp"),
        ),
        out_specs=(
            P(("dp", "expert"), None),
            P(("dp", "expert"), None),
            P(("dp", "expert"), None),
            P("expert", "dp", None),
            P("expert", "dp", None),
            P("expert", None, "dp"),
        ),
        check_vma=False,
    )
```

```python
import functools

import jax
import jax.numpy as jnp
import numpy as np
from jax import lax
from jax.experimental import pallas as pl
from jax.experimental.pallas import tpu as pltpu
from jax.sharding import PartitionSpec as P

LANES = 128
F32 = jnp.float32
BF16 = jnp.bfloat16
VMEM = pl.BlockSpec(memory_space=pltpu.VMEM)
SMEM = pl.BlockSpec(memory_space=pltpu.SMEM)


def grant(mib):
    return pltpu.CompilerParams(vmem_limit_bytes=mib << 20)


def neighbour(i, dx, dz, dc):
    z, x, c = i // 8, i // 2 % 4, i % 2
    return ((z ^ dz) * 4 + (x + dx) % 4) * 2 + (c ^ dc)


BLOCKS = [(dc, dz, dx) for dc in range(2) for dz in range(2) for dx in range(4)]


def push(value, dx=0, dz=0, dc=0):
    return lax.ppermute(value, "dp", [(i, neighbour(i, dx, dz, dc)) for i in range(16)])


def z_target(dp, expert, turn):
    shift = (0, 1, -2 if dp % 2 else 2, -1)[turn]
    z = (dp // 8 * 4 + expert % 4 + shift) % 8
    return z // 4 * 8 + dp % 8, expert // 4 * 4 + z % 4


def z_pairs(turn):
    pairs = []
    for i in range(256):
        dp, expert = z_target(i // 16, i % 16, turn)
        pairs.append((i, dp * 16 + expert))
    return pairs


def z_send(value, turn):
    return lax.ppermute(value, ("dp", "expert"), z_pairs(turn))


def z_return(value, turn):
    return lax.ppermute(value, ("dp", "expert"), [(j, i) for i, j in z_pairs(turn)])


def y_send(value, dy):
    return lax.ppermute(value, "expert", [(i, (i + 4 * dy) % 16) for i in range(16)])


def column_spots():
    spots = np.zeros((16, 16), np.int32)
    for i in range(16):
        for j, block in enumerate(BLOCKS):
            spots[i, neighbour(i, *reversed(block))] = j
    table = np.zeros((256, 4, 16), np.int32)
    for i in range(256):
        for turn in range(4):
            table[i, turn] = spots[z_target(i // 16, i % 16, turn)[0]]
    return jnp.array(table)[lax.axis_index("dp") * 16 + lax.axis_index("expert")]


def add(*values):
    total = values[0].astype(F32)
    for value in values[1:]:
        total = total + value.astype(F32)
    return total


def block_cols(j):
    return slice(j * LANES, (j + 1) * LANES)


def spot(spots, turn, j):
    return pl.ds(pl.multiple_of(spots[turn, j] * LANES, LANES), LANES)


def place_in_buffer(me, cap, experts, routes):
    tokens = routes.shape[1]
    lanes = [routes[k : k + 1, :] for k in range(2)]
    kinds = lax.broadcasted_iota(jnp.int32, (experts, tokens), 0)
    hits = [(kinds == lane).astype(F32) for lane in lanes]
    earlier = lax.broadcasted_iota(jnp.int32, (tokens, tokens), 0) < lax.broadcasted_iota(
        jnp.int32, (tokens, tokens), 1
    )
    counts = jnp.dot(
        (hits[0] + hits[1]).astype(BF16),
        earlier.astype(F32).astype(BF16),
        preferred_element_type=F32,
    )
    targets = []
    for k in range(2):
        slot = jnp.sum(counts * hits[k], axis=0, keepdims=True).astype(jnp.int32)
        turns, steps = (lanes[k] - me) & 3, ((lanes[k] >> 2) - (me >> 2)) & 3
        targets.append((turns * 4 + steps) * cap + slot)
    return targets


def send_kernel(scaled, cap, experts, spots, me, routes, gates, rows, *outs):
    targets = place_in_buffer(me[0], cap, experts, routes[...])
    spots_of = lax.broadcasted_iota(jnp.int32, (experts * cap, rows.shape[0]), 0)
    hits = [spots_of == target for target in targets]
    pick = jnp.where(hits[0] | hits[1], 1.0, 0.0).astype(BF16)
    if scaled:
        weight = jnp.where(hits[0], gates[0:1, :], 0.0) + jnp.where(hits[1], gates[1:2, :], 0.0)
        row_gate = jnp.sum(weight, axis=1, keepdims=True)
    else:
        outs[4][0:1, :], outs[4][1:2, :] = targets
    for j in range(4):
        moved = jnp.dot(pick, rows[:, j * 512 : (j + 1) * 512], preferred_element_type=F32)
        if scaled:
            moved = moved * row_gate
        moved = moved.astype(BF16)
        for i in range(4):
            for turn in range(4):
                cols = spot(spots, turn, j * 4 + i)
                for step in range(4):
                    row = (turn * 4 + step) * cap
                    outs[step][turn * cap : (turn + 1) * cap, cols] = moved[
                        row : row + cap, block_cols(i)
                    ]


def send(scaled, spots, routes, gates, rows):
    (tokens, width), experts = rows.shape, lax.axis_size("expert")
    cap = tokens * routes.shape[0] * 2 // experts
    slots = experts * cap
    shapes = [jax.ShapeDtypeStruct((slots // 4, width), BF16)] * 4
    if not scaled:
        shapes = shapes + [jax.ShapeDtypeStruct(routes.shape, jnp.int32)]
    return pl.pallas_call(
        functools.partial(send_kernel, scaled, cap, experts),
        out_shape=shapes,
        in_specs=[SMEM] * 2 + [VMEM] * 3,
        out_specs=[VMEM] * len(shapes),
        cost_estimate=pl.CostEstimate(
            flops=2 * slots * tokens * width, bytes_accessed=3 * slots * width, transcendentals=0
        ),
        name="send",
        compiler_params=grant(7),
    )(spots, lax.axis_index("expert").reshape(1), routes, gates, rows)


def turn_kernel(b0, b1, b2, b3, *outs):
    size = b0.shape[0] // 4
    for i, block in enumerate((b0, b1, b2, b3)):
        for k in range(4):
            outs[k][i * size : (i + 1) * size] = block[k * size : (k + 1) * size]


def turn_blocks(blocks):
    return pl.pallas_call(
        turn_kernel,
        out_shape=[jax.ShapeDtypeStruct(blocks[0].shape, BF16)] * 4,
        in_specs=[VMEM] * 4,
        out_specs=[VMEM] * 4,
        cost_estimate=pl.CostEstimate(
            flops=0, bytes_accessed=16 * blocks[0].size, transcendentals=0
        ),
        name="turn",
        compiler_params=grant(6),
    )(*blocks)


NT = (((1,), (1,)), ((), ()))
TN = (((0,), (0,)), ((), ()))


def chunk(n, size):
    return pl.ds(pl.multiple_of(n * size, size), size)


def quarter_dot(a, quarters, where):
    depth = quarters[0].shape[0]
    total = None
    for q, w in enumerate(quarters):
        part = jnp.dot(
            a[:, q * depth : (q + 1) * depth], w[:, where], preferred_element_type=F32
        )
        total = part if total is None else total + part
    return total


def forward_kernel(b0, b1, b2, b3, w0, w1, w2, w3, x_in, hidden, act, slope, *outs):
    size, hid = b0.shape[0], hidden.shape[1]
    quarters = (w0, w1, w2, w3)
    for k, block in enumerate((b0, b1, b2, b3)):
        x_in[k * size : (k + 1) * size] = block[...]

    @pl.loop(0, hid // 256)
    def _(n):
        cols, up_cols = chunk(n, 256), pl.ds(pl.multiple_of(hid + n * 256, 256), 256)
        pre, up = quarter_dot(x_in, quarters, cols), quarter_dot(x_in, quarters, up_cols)
        sig = jax.nn.sigmoid(pre)
        silu = pre * sig
        act[:, cols] = silu.astype(BF16)
        slope[:, cols] = (up * sig * (1.0 + pre * (1.0 - sig))).astype(BF16)
        hidden[:, cols] = (silu * up).astype(BF16)

    cap = size // 4
    for q, w in enumerate(quarters):
        cols = slice(q * 512, (q + 1) * 512)
        rows = lax.dot_general(
            hidden[...], w[:, 2 * hid :], NT, preferred_element_type=F32
        ).astype(BF16)
        for turn in range(4):
            for step in range(4):
                row = (turn * 4 + step) * cap
                outs[step][turn * cap : (turn + 1) * cap, cols] = rows[row : row + cap]


def forward(blocks, quarters, hid):
    rows, width = blocks[0].shape
    whole = 4 * rows
    return pl.pallas_call(
        forward_kernel,
        out_shape=[jax.ShapeDtypeStruct((whole, width), BF16)]
        + [jax.ShapeDtypeStruct((whole, hid), BF16)] * 3
        + [jax.ShapeDtypeStruct((rows, width), BF16)] * 4,
        in_specs=[VMEM] * 8,
        out_specs=[VMEM] * 8,
        cost_estimate=pl.CostEstimate(
            flops=6 * whole * width * hid,
            bytes_accessed=6 * width * hid + 6 * whole * width + 6 * whole * hid,
            transcendentals=whole * hid,
        ),
        name="forward",
        compiler_params=grant(22),
    )(*blocks, *quarters)


def hidden_kernel(b0, b1, b2, b3, w0, w1, w2, w3, act, slope, d_in, d_both):
    size, hid = b0.shape[0], act.shape[1]
    for k, block in enumerate((b0, b1, b2, b3)):
        d_in[k * size : (k + 1) * size] = block[...]

    @pl.loop(0, hid // 256)
    def _(n):
        cols, up_cols = chunk(n, 256), pl.ds(pl.multiple_of(hid + n * 256, 256), 256)
        d_hidden = quarter_dot(d_in, (w0, w1, w2, w3), cols)
        d_both[:, cols] = (d_hidden * slope[:, cols].astype(F32)).astype(BF16)
        d_both[:, up_cols] = (d_hidden * act[:, cols].astype(F32)).astype(BF16)


def whole_spec(shape):
    return pl.BlockSpec(shape, lambda *_: (0,) * len(shape))


def hidden_grads(blocks, quarters, act, slope):
    (rows, width), (whole, hid) = blocks[0].shape, act.shape
    return pl.pallas_call(
        hidden_kernel,
        grid=(1,),
        out_shape=[
            jax.ShapeDtypeStruct((whole, width), BF16),
            jax.ShapeDtypeStruct((whole, 2 * hid), BF16),
        ],
        in_specs=[whole_spec((rows, width))] * 4
        + [pl.BlockSpec((width // 4, hid), lambda i: (0, 2))] * 4
        + [whole_spec((whole, hid))] * 2,
        out_specs=[whole_spec((whole, width)), whole_spec((whole, 2 * hid))],
        cost_estimate=pl.CostEstimate(
            flops=2 * whole * width * hid,
            bytes_accessed=2 * width * hid + 4 * whole * width + 8 * whole * hid,
            transcendentals=0,
        ),
        name="hidden_grads",
        compiler_params=grant(14),
    )(*blocks, *quarters, act, slope)


def row_grads_kernel(d_both, w0, w1, w2, w3, *outs):
    size = outs[0].shape[0]
    for q, w in enumerate((w0, w1, w2, w3)):
        rows = lax.dot_general(d_both[...], w[...], NT, preferred_element_type=F32).astype(BF16)
        for k in range(4):
            outs[k][:, q * 512 : (q + 1) * 512] = rows[k * size : (k + 1) * size]


def row_grads(d_both, quarters):
    (whole, both), width = d_both.shape, 4 * quarters[0].shape[0]
    return pl.pallas_call(
        row_grads_kernel,
        grid=(1,),
        out_shape=[jax.ShapeDtypeStruct((whole // 4, width), BF16)] * 4,
        in_specs=[whole_spec((whole, both))]
        + [pl.BlockSpec((width // 4, both), lambda i: (0, 0))] * 4,
        out_specs=[whole_spec((whole // 4, width))] * 4,
        cost_estimate=pl.CostEstimate(
            flops=2 * whole * width * both,
            bytes_accessed=2 * (width * both + whole * width + whole * both),
            transcendentals=0,
        ),
        name="row_grads",
        compiler_params=grant(13),
    )(d_both, *quarters)


def weight_grads_kernel(base, x_in, d_in, d_both, hidden, *refs):
    def put(value):
        if len(refs) == 1:
            refs[0][...] = value.astype(BF16)
        else:
            value = (value + refs[0][...].astype(F32)).astype(BF16)
            for i, out in enumerate(refs[1:]):
                out[...] = value[i * LANES : (i + 1) * LANES]

    @pl.when(pl.program_id(0) < 2)
    def _():
        put(lax.dot_general(x_in[...], d_both[...], TN, preferred_element_type=F32))

    @pl.when(pl.program_id(0) == 2)
    def _():
        put(lax.dot_general(d_in[...], hidden[...], TN, preferred_element_type=F32))


def weight_grads(quarter, x_in, d_in, d_both, hidden, came=None):
    (whole, width), hid = x_in.shape, hidden.shape[1]
    size = width // 4
    columns = pl.BlockSpec((whole, size), lambda n, base: (0, base[0]))
    third = pl.BlockSpec((size, hid), lambda n, base: (0, n))
    inputs = [x_in, d_in, d_both, hidden]
    specs = [
        columns,
        columns,
        pl.BlockSpec((whole, hid), lambda n, base: (0, jnp.minimum(n, 1))),
        pl.BlockSpec((whole, hid), lambda n, base: (0, 0)),
    ]
    shape, out = jax.ShapeDtypeStruct((size, 3 * hid), BF16), third
    if came is not None:
        inputs, specs = inputs + [came], specs + [third]
        shape = [jax.ShapeDtypeStruct((LANES, 3 * hid), BF16)] * 4
        out = [pl.BlockSpec((LANES, hid), lambda n, base: (0, n))] * 4
    return pl.pallas_call(
        weight_grads_kernel,
        grid_spec=pltpu.PrefetchScalarGridSpec(
            num_scalar_prefetch=1, grid=(3,), in_specs=specs, out_specs=out
        ),
        out_shape=shape,
        cost_estimate=pl.CostEstimate(
            flops=6 * whole * size * hid,
            bytes_accessed=4 * whole * size + 6 * whole * hid + 6 * size * hid,
            transcendentals=0,
        ),
        name="weight_grads",
        compiler_params=grant(10),
    )(jnp.full((1,), quarter, jnp.int32), *inputs)


def picks(targets, slots):
    rows = lax.broadcasted_iota(jnp.int32, (slots, targets.shape[1]), 0)
    return [rows == targets[k : k + 1, :] for k in range(2)]


def gather_back(spots, blocks, back):
    cap = blocks[0].shape[0] // 4
    for step, block in enumerate(blocks):
        for turn in range(4):
            row = (turn * 4 + step) * cap
            for j in range(16):
                back[row : row + cap, block_cols(j)] = block[
                    turn * cap : (turn + 1) * cap, spot(spots, turn, j)
                ]


def combine_kernel(spots, targets, gates, b0, b1, b2, b3, cotangent, out, grad_gates, back):
    size = b0.shape[0]
    for turn, block in enumerate((b0, b1, b2, b3)):
        for j in range(16):
            back[turn * size : (turn + 1) * size, block_cols(j)] = block[:, spot(spots, turn, j)]
    tokens = out.shape[0]
    first, second = [
        jnp.where(hit, 1.0, 0.0).astype(BF16) for hit in picks(targets[...], back.shape[0])
    ]
    g0, g1 = gates[:, 0:1], gates[:, 1:2]
    s0 = jnp.zeros((tokens, LANES), F32)
    s1 = jnp.zeros((tokens, LANES), F32)
    for j in range(4):
        cols = slice(j * 512, (j + 1) * 512)
        o0 = lax.dot_general(first, back[:, cols], TN, preferred_element_type=F32)
        o1 = lax.dot_general(second, back[:, cols], TN, preferred_element_type=F32)
        out[:, cols] = (g0 * o0 + g1 * o1).astype(BF16)
        dy = cotangent[:, cols].astype(F32)
        t0, t1 = o0 * dy, o1 * dy
        for i in range(4):
            s0 = s0 + t0[:, block_cols(i)]
            s1 = s1 + t1[:, block_cols(i)]
    grad_gates[:, 0:1] = jnp.sum(s0, axis=1, keepdims=True)
    grad_gates[:, 1:2] = jnp.sum(s1, axis=1, keepdims=True)


def combine(spots, targets, gates, blocks, cotangent):
    (rows, width), slots = cotangent.shape, 4 * blocks[0].shape[0]
    return pl.pallas_call(
        combine_kernel,
        out_shape=[
            jax.ShapeDtypeStruct((rows, width), BF16),
            jax.ShapeDtypeStruct(gates.shape, F32),
        ],
        in_specs=[SMEM] + [VMEM] * 7,
        out_specs=[VMEM] * 2,
        scratch_shapes=[pltpu.VMEM((slots, width), BF16)],
        cost_estimate=pl.CostEstimate(
            flops=4 * slots * rows * width, bytes_accessed=2 * slots * width * 2, transcendentals=0
        ),
        name="combine",
        compiler_params=grant(10),
    )(spots, targets, gates, *blocks, cotangent)


def grad_tokens_kernel(spots, targets, b0, b1, b2, b3, out, back):
    gather_back(spots, (b0, b1, b2, b3), back)
    hits = picks(targets[...], back.shape[0])
    pick = jnp.where(hits[0] | hits[1], 1.0, 0.0).astype(BF16)
    for j in range(4):
        cols = slice(j * 512, (j + 1) * 512)
        out[:, cols] = lax.dot_general(
            pick, back[:, cols], TN, preferred_element_type=F32
        ).astype(BF16)


def combine_grads(spots, targets, blocks):
    width, slots, rows = blocks[0].shape[1], 4 * blocks[0].shape[0], targets.shape[1]
    return pl.pallas_call(
        grad_tokens_kernel,
        out_shape=jax.ShapeDtypeStruct((rows, width), BF16),
        in_specs=[SMEM] + [VMEM] * 5,
        out_specs=VMEM,
        scratch_shapes=[pltpu.VMEM((slots, width), BF16)],
        cost_estimate=pl.CostEstimate(
            flops=2 * slots * rows * width, bytes_accessed=2 * slots * width * 2, transcendentals=0
        ),
        name="grad_tokens",
        compiler_params=grant(8),
    )(spots, targets, *blocks)


def over_z(mover, blocks):
    return [blocks[0]] + [mover(blocks[turn], turn) for turn in range(1, 4)]


def over_x(block):
    return jnp.concatenate([block] + [push(block, dx=-dx) for dx in (1, 2, 3)], axis=0)


def over_y(sign, blocks):
    return [blocks[0]] + [y_send(blocks[dy], sign * dy) for dy in range(1, 4)]


def shards(tokens, routes, gates, cotangent, w_gate, w_up, w_down):
    hid = w_gate.shape[2]
    spots = column_spots()
    routes_t, gates_t = routes.T, gates.T

    own = jnp.concatenate([w_gate[0], w_up[0], w_down[0].T], axis=1)
    far = push(own, dz=1)

    *x_met, targets = send(False, spots, routes_t, gates_t, tokens)
    x_met = over_y(1, x_met)
    d_met = send(True, spots, routes_t, gates_t, cotangent)
    d_met = over_y(1, d_met)

    first = over_x(own)
    second = over_x(far)
    first_other = push(first, dc=1)
    second_other = push(second, dc=1)
    quarters = first, second, first_other, second_other

    x_met = turn_blocks(x_met)
    x_blocks = over_z(z_send, x_met)
    d_met = turn_blocks(d_met)
    d_blocks = over_z(z_send, d_met)

    x_in, hidden, act, slope, *o_sent = forward(x_blocks, quarters, hid)
    o_met = over_y(-1, o_sent)
    d_in, d_both = hidden_grads(d_blocks, quarters, act, slope)
    saved = x_in, d_in, d_both, hidden

    came1 = weight_grads(3, *saved)
    came1 = push(came1, dc=1)
    came0 = weight_grads(2, *saved)
    came0 = push(came0, dc=1)

    def sum_over_x(dz, came):
        mine, *rest = weight_grads(dz, *saved, came)
        met = [push(rest[dx - 1], dx=dx) for dx in (1, 2, 3)]
        return add(mine, *met)

    far_sum = sum_over_x(1, came1).astype(BF16)
    far_sum = push(far_sum, dz=1)
    r_sent = row_grads(d_both, quarters)
    r_met = over_z(z_return, r_sent)
    grads = add(sum_over_x(0, came0), far_sum).astype(BF16)

    o_met = turn_blocks(o_met)
    o_blocks = over_z(z_return, o_met)
    r_met = turn_blocks(r_met)
    r_blocks = over_y(-1, r_met)
    output, grad_gates = combine(spots, targets, gates, o_blocks, cotangent)
    grad_tokens = combine_grads(spots, targets, r_blocks)
    return (
        output,
        grad_tokens,
        grad_gates,
        grads[None, :, :hid],
        grads[None, :, hid : 2 * hid],
        grads[:, 2 * hid :].T[None],
    )


def solution(mesh):
    return jax.shard_map(
        shards,
        mesh=mesh,
        in_specs=(
            P(("dp", "expert"), None),
            P(("dp", "expert"), None),
            P(("dp", "expert"), None),
            P(("dp", "expert"), None),
            P("expert", "dp", None),
            P("expert", "dp", None),
            P("expert", None, "dp"),
        ),
        out_specs=(
            P(("dp", "expert"), None),
            P(("dp", "expert"), None),
            P(("dp", "expert"), None),
            P("expert", "dp", None),
            P("expert", "dp", None),
            P("expert", None, "dp"),
        ),
        check_vma=False,
    )
```
